512 devices in a mesh: uly: 16 (over y, z_hi), blk: 32 (over z_lo, x, core).
Axes of the slice: x: 4, y: 4, z: 16 (z_hi: 4, z_lo: 4; z = z_hi * 4 + z_lo), core: 2. Of those that a mesh axis runs over, the one named last changes fastest.
Arguments:
- queries: bfloat16 [65536, 2048], P(('blk', 'uly')), may hold values from -6 to 6
- key_projection: bfloat16 [65536, 256], P(('blk', 'uly')), may hold values from -6 to 6
- value_projection: bfloat16 [65536, 256], P(('blk', 'uly')), may hold values from -6 to 6
- output_gradient: bfloat16 [65536, 2048], P(('blk', 'uly')), may hold values from -6 to 6
- doc_lengths: int32 [64], replicated, may hold values from 1 to 2048, 65536 in all
Outputs:
- context: bfloat16 [65536, 2048], P(('blk', 'uly'))
- grad_queries: bfloat16 [65536, 2048], P(('blk', 'uly'))
- keys_gradient: bfloat16 [65536, 256], P(('blk', 'uly'))
- values_gradient: bfloat16 [65536, 256], P(('blk', 'uly'))
The draws below stay inside these ranges and needn't reach their ends.
Inputs may be any that keep to these rules, and one draw needn't show every extreme that they name: `doc_lengths`: the 64 lengths sum to 65536, and the longest is exactly 2048.
All inputs are finite; a program needn't handle non-finite values.
Results may differ from the reference program's by a relative error of at most 0.011.
Values may be sent and summed in bfloat16 or wider, within the bound.
No kernel may reach another device: no remote copies, remote signals or barrier semaphores. Data moves between devices by JAX's collectives and lax.ppermute only.
A program may use at most 64 MiB of HBM per device.

```python
import math
import jax
import jax.numpy as jnp
import numpy as np
from jax import lax

QUERY_HEADS = 16
KEY_VALUE_HEADS = 2
HEAD_SIZE = 128
PACKED_TOKENS = 65536
LONGEST_DOC = 2048
DOCS = 64


def draw_key_projection(key, part):
    pattern_key = jax.random.fold_in(key, 3)
    final_result = jnp.clip(jax.random.normal(pattern_key, (PACKED_TOKENS, KEY_VALUE_HEADS, HEAD_SIZE), jnp.float32), -5.0, 5.0)
    return final_result.reshape(PACKED_TOKENS, KEY_VALUE_HEADS * HEAD_SIZE).astype(jnp.bfloat16)


def draw_queries(key, part):
    pattern_key = jax.random.fold_in(key, 5)
    final_result = jnp.clip(jax.random.normal(pattern_key, (PACKED_TOKENS, QUERY_HEADS, HEAD_SIZE), jnp.float32), -5.0, 5.0)
    return final_result.reshape(PACKED_TOKENS, QUERY_HEADS * HEAD_SIZE).astype(jnp.bfloat16)


def shard_levels(rng, dims, shards, least, top_value):
    gain, own = 1.0, jax.random.fold_in(rng, 6)
    for axis_at, blocks in shards:
        heights = jnp.exp(jax.random.uniform(jax.random.fold_in(own, axis_at), (blocks,), jnp.float32, least / len(shards), top_value / len(shards)))
        gain = gain * jnp.repeat(heights, dims[axis_at] // blocks).reshape([-1 if axis == axis_at else 1 for axis in range(len(dims))])
    return gain


def length_profile(count, total, limit, skew):
    loads = [(1 << 20) // math.isqrt(standing ** skew) + 1 for standing in range(2, count + 1)]
    spare, given = total - limit - (count - 1), [1] * (count - 1)
    while spare > 0:
        candidates = [i for i in range(count - 1) if given[i] < limit]
        mass, budget = sum([loads[i] for i in candidates]), spare
        for i in candidates:
            extra = min(limit - given[i], max(1, budget * loads[i] // mass), spare)
            given[i] = given[i] + extra
            spare = spare - extra
    return np.array([limit] + given)


def uneven_parts(rng, count, total, limit, lean):
    if count == 2:
        one = jax.random.randint(rng, (), max(1, total - limit), min(limit, total - 1) + 1)
        return jnp.stack([one, total - one])
    tallies = jnp.asarray(length_profile(count, total, limit, lean), jnp.int32)
    twos = (count - 1) // 2
    donor, receiver = tallies[1:1 + 2 * twos:2], tallies[2:2 + 2 * twos:2]
    slack = jnp.minimum(donor - 1, limit - receiver)
    passed = jax.random.randint(jax.random.fold_in(rng, 1), (twos,), 0, 1 << 20) % (slack + 1)
    tallies = tallies.at[1:1 + 2 * twos:2].set(donor - passed).at[2:2 + 2 * twos:2].set(receiver + passed)
    return tallies[jax.random.permutation(jax.random.fold_in(rng, 2), count)]


def bell_draw(stream_key, shape, spread, limit, pieces=(), held_as=jnp.bfloat16):
    gain = shard_levels(stream_key, shape, pieces, -0.22, 0.18) if pieces else 1.0
    drawn = jax.random.normal(stream_key, shape, jnp.float32) * spread * gain
    return jnp.minimum(jnp.maximum(drawn, -limit), limit).astype(held_as)


def setup_inputs(seed: int = 0) -> dict:
    splits = jax.random.split(jax.random.key(seed), 6)
    return {
        "queries": draw_queries(jax.random.fold_in(splits[5], 71), 0),
        "key_projection": draw_key_projection(jax.random.fold_in(splits[5], 71), 0),
        "value_projection": bell_draw(splits[2], (PACKED_TOKENS, KEY_VALUE_HEADS * HEAD_SIZE), 1.0, 6.0, ((0, 512),)),
        "output_gradient": bell_draw(splits[3], (PACKED_TOKENS, QUERY_HEADS * HEAD_SIZE), 1.0, 6.0, ((0, 512),)),
        "doc_lengths": uneven_parts(splits[4], DOCS, PACKED_TOKENS, LONGEST_DOC, 2).astype(jnp.int32),
    }


def reference(queries, key_projection, value_projection, output_gradient, doc_lengths):
    group_width = QUERY_HEADS // KEY_VALUE_HEADS
    logit_scale = 1.0 / math.sqrt(HEAD_SIZE)
    block_rows = min(512, PACKED_TOKENS)
    span_window = LONGEST_DOC + block_rows
    doc_ends = jnp.cumsum(doc_lengths).astype(jnp.int32)
    doc_starts = (doc_ends - doc_lengths).astype(jnp.int32)
    pad_amount = jnp.zeros((LONGEST_DOC, KEY_VALUE_HEADS * HEAD_SIZE), jnp.bfloat16)
    padded_key_rows = jnp.concatenate([pad_amount, key_projection], axis=0)
    padded_value_rows = jnp.concatenate([pad_amount, value_projection], axis=0)

    def tile_body(carried, tile_index):
        grad_key_acc, grad_value_acc = carried
        start_shift = (tile_index * block_rows).astype(jnp.int32)
        query_block = lax.dynamic_slice_in_dim(queries, start_shift, block_rows, 0).reshape(block_rows, KEY_VALUE_HEADS, group_width, HEAD_SIZE).astype(jnp.float32)
        gradient_block = lax.dynamic_slice_in_dim(output_gradient, start_shift, block_rows, 0).reshape(block_rows, KEY_VALUE_HEADS, group_width, HEAD_SIZE).astype(jnp.float32)
        key_block = lax.dynamic_slice_in_dim(padded_key_rows, start_shift, span_window, 0).reshape(span_window, KEY_VALUE_HEADS, HEAD_SIZE).astype(jnp.float32)
        value_block = lax.dynamic_slice_in_dim(padded_value_rows, start_shift, span_window, 0).reshape(span_window, KEY_VALUE_HEADS, HEAD_SIZE).astype(jnp.float32)
        query_pos = start_shift + jnp.arange(block_rows, dtype=jnp.int32)
        key_pos = start_shift - LONGEST_DOC + jnp.arange(span_window, dtype=jnp.int32)
        doc_begin = lax.optimization_barrier(jnp.max(jnp.where(doc_starts[None, :] <= query_pos[:, None], doc_starts[None, :], 0), axis=1))
        allowed = (key_pos[None, :] <= query_pos[:, None]) & (key_pos[None, :] >= doc_begin[:, None])
        scores = jnp.einsum('qhgd,khd->hgqk', query_block, key_block) * logit_scale
        masked = jnp.where(allowed, scores, -jnp.inf)
        row_top = lax.optimization_barrier(jnp.max(masked, axis=3, keepdims=True))
        log_total = row_top + jnp.log(lax.optimization_barrier(jnp.sum(jnp.exp(masked - row_top), axis=3, keepdims=True)))
        weights = jnp.where(allowed, jnp.exp(scores - log_total), 0.0)
        weight_narrow = lax.optimization_barrier(weights.astype(jnp.bfloat16)).astype(jnp.float32)
        attended = jnp.einsum('hgqk,khd->qhgd', weight_narrow, value_block)
        row_delta = jnp.einsum('qhgd,qhgd->hgq', gradient_block, attended)
        grad_weights = jnp.einsum('qhgd,khd->hgqk', gradient_block, value_block)
        grad_scores = weights * (grad_weights - row_delta[..., None])
        score_gradient_narrow = lax.optimization_barrier(grad_scores.astype(jnp.bfloat16)).astype(jnp.float32)
        grad_query = logit_scale * jnp.einsum('hgqk,khd->qhgd', score_gradient_narrow, key_block)
        key_gradient = logit_scale * jnp.einsum('bnwr,wbno->rbo', score_gradient_narrow, query_block).reshape(span_window, KEY_VALUE_HEADS * HEAD_SIZE)
        value_gradient = jnp.einsum('bnwr,wbno->rbo', weight_narrow, gradient_block).reshape(span_window, KEY_VALUE_HEADS * HEAD_SIZE)
        grad_key_acc = lax.dynamic_update_slice_in_dim(grad_key_acc, lax.dynamic_slice_in_dim(grad_key_acc, start_shift, span_window, 0) + key_gradient, start_shift, 0)
        grad_value_acc = lax.dynamic_update_slice_in_dim(grad_value_acc, lax.dynamic_slice_in_dim(grad_value_acc, start_shift, span_window, 0) + value_gradient, start_shift, 0)
        return ((grad_key_acc, grad_value_acc), (attended.reshape(block_rows, QUERY_HEADS * HEAD_SIZE).astype(jnp.bfloat16), grad_query.reshape(block_rows, QUERY_HEADS * HEAD_SIZE).astype(jnp.bfloat16)))
    starting_carry = jnp.zeros((PACKED_TOKENS + LONGEST_DOC, KEY_VALUE_HEADS * HEAD_SIZE), jnp.float32)
    (grad_key_acc, grad_value_acc), (context, grad_queries) = lax.scan(tile_body, (starting_carry, starting_carry), jnp.arange(PACKED_TOKENS // block_rows, dtype=jnp.int32))
    context = context.reshape(PACKED_TOKENS, QUERY_HEADS * HEAD_SIZE)
    grad_queries = grad_queries.reshape(PACKED_TOKENS, QUERY_HEADS * HEAD_SIZE)
    keys_gradient = grad_key_acc[LONGEST_DOC:].astype(jnp.bfloat16)
    values_gradient = grad_value_acc[LONGEST_DOC:].astype(jnp.bfloat16)
    return (context, grad_queries, keys_gradient, values_gradient)
```

```python
import math

import jax
import jax.numpy as jnp
import numpy as np
from jax import lax
from jax.experimental import pallas as pl
from jax.experimental.pallas import tpu as pltpu
from jax.sharding import Mesh
from jax.sharding import PartitionSpec as P

HEAD_SIZE = 128
SPAN = 2048
CHUNK = 128
TILE = 256
TILES = 2 * SPAN // TILE
OWN = SPAN // TILE
HEADS = 4
ROWS = HEADS * CHUNK
BLOCK_AXES = ("z_lo", "x", "core")
TOKEN_AXES = ("z_lo", "x", "core", "y", "z_hi")
SCALE = 1.0 / math.sqrt(HEAD_SIZE)
LOG2_SCALE = SCALE * math.log2(math.e)


def attention_kernel(
    scalars, begin_ref, qd_ref, kv_before_ref, kv_own_ref,
    out_ref, grad_before_ref, grad_own_ref,
    keys, values, keys_t, values_t, probs, grad_keys, grad_values, out_t, grad_query_t, top, total,
):
    first = scalars[0]
    z_hi = scalars[4]

    def load(source, shift):
        def body(tile, _):
            both = source[tile - shift]
            k, v = both[:, :HEAD_SIZE], both[:, HEAD_SIZE:]
            keys[tile] = k
            values[tile] = v
            keys_t[tile] = k.T
            values_t[tile] = v.T
            return 0

        return body

    lax.fori_loop(first, OWN, load(kv_before_ref, 0), 0)
    lax.fori_loop(jnp.maximum(first, OWN), TILES, load(kv_own_ref, OWN), 0)

    def clear(tile, _):
        grad_keys[tile] = jnp.zeros((TILE, HEAD_SIZE), jnp.float32)
        grad_values[tile] = jnp.zeros((TILE, HEAD_SIZE), jnp.float32)
        return 0

    lax.fori_loop(0, TILES, clear, 0)

    def chunk_step(chunk, _):
        start = SPAN + (4 * chunk + z_hi) * CHUNK
        low = scalars[chunk]
        high = (start + CHUNK - 1) // TILE + 1
        block = qd_ref[chunk]
        rows_q = jnp.concatenate(
            [block[:CHUNK, h * HEAD_SIZE : (h + 1) * HEAD_SIZE] for h in range(HEADS)], axis=0
        )
        rows_d = jnp.concatenate(
            [block[CHUNK:, h * HEAD_SIZE : (h + 1) * HEAD_SIZE] for h in range(HEADS)], axis=0
        )
        query_pos = start + (lax.broadcasted_iota(jnp.int32, (1, ROWS), 1) & (CHUNK - 1))
        begin = begin_ref[chunk]
        top[...] = jnp.full((8, ROWS), -1e30, jnp.float32)
        total[...] = jnp.zeros((8, ROWS), jnp.float32)
        out_t[...] = jnp.zeros((HEAD_SIZE, ROWS), jnp.float32)
        grad_query_t[...] = jnp.zeros((HEAD_SIZE, ROWS), jnp.float32)

        def scores_step(tile, _):
            s = lax.dot_general(
                keys[tile], rows_q, (((1,), (1,)), ((), ())), preferred_element_type=jnp.float32
            )
            key_pos = tile * TILE + lax.broadcasted_iota(jnp.int32, (TILE, ROWS), 0)
            allowed = (key_pos >= begin) & (key_pos <= query_pos)
            s = jnp.where(allowed, s * LOG2_SCALE, -1e30)
            probs[tile] = s
            top[...] = jnp.maximum(top[...], jnp.max(s.reshape(TILE // 8, 8, ROWS), axis=0))
            return 0

        lax.fori_loop(low, high, scores_step, 0)
        row_top = jnp.max(top[...], axis=0, keepdims=True)

        def output_step(tile, _):
            p = jnp.exp2(probs[tile] - row_top)
            probs[tile] = p
            total[...] += jnp.sum(p.reshape(TILE // 8, 8, ROWS), axis=0)
            out_t[...] += lax.dot_general(
                values_t[tile], p.astype(jnp.bfloat16), (((1,), (0,)), ((), ())),
                preferred_element_type=jnp.float32,
            )
            return 0

        lax.fori_loop(low, high, output_step, 0)
        inverse = 1.0 / jnp.sum(total[...], axis=0, keepdims=True)
        attended = out_t[...] * inverse
        context = attended.T
        delta = jnp.sum(rows_d.astype(jnp.float32).T * attended, axis=0, keepdims=True)

        def gradient_step(tile, _):
            w = probs[tile] * inverse
            grad_weights = lax.dot_general(
                values[tile], rows_d, (((1,), (1,)), ((), ())), preferred_element_type=jnp.float32
            )
            grad_scores = (w * (grad_weights - delta)).astype(jnp.bfloat16)
            grad_values[tile] += lax.dot_general(
                w.astype(jnp.bfloat16), rows_d, (((1,), (0,)), ((), ())),
                preferred_element_type=jnp.float32,
            )
            grad_keys[tile] += lax.dot_general(
                grad_scores, rows_q, (((1,), (0,)), ((), ())), preferred_element_type=jnp.float32
            )
            grad_query_t[...] += lax.dot_general(
                keys_t[tile], grad_scores, (((1,), (0,)), ((), ())),
                preferred_element_type=jnp.float32,
            )
            return 0

        lax.fori_loop(low, high, gradient_step, 0)
        grad_query = (grad_query_t[...] * SCALE).T
        for h in range(HEADS):
            span = slice(h * HEAD_SIZE, (h + 1) * HEAD_SIZE)
            out_ref[chunk, :CHUNK, span] = context[h * CHUNK : (h + 1) * CHUNK].astype(jnp.bfloat16)
            out_ref[chunk, CHUNK:, span] = grad_query[h * CHUNK : (h + 1) * CHUNK].astype(jnp.bfloat16)
        return 0

    lax.fori_loop(0, 4, chunk_step, 0)

    def store(target, shift):
        def body(tile, _):
            target[tile - shift, :, :HEAD_SIZE] = (grad_keys[tile] * SCALE).astype(jnp.bfloat16)
            target[tile - shift, :, HEAD_SIZE:] = grad_values[tile].astype(jnp.bfloat16)
            return 0

        return body

    lax.fori_loop(0, OWN, store(grad_before_ref, 0), 0)
    lax.fori_loop(OWN, TILES, store(grad_own_ref, OWN), 0)


def attention(scalars, begin, qd, kv_before, kv_own):
    vmem = pl.BlockSpec(memory_space=pltpu.VMEM)
    tiles = jax.ShapeDtypeStruct((OWN, TILE, 2 * HEAD_SIZE), jnp.bfloat16)
    f32, bf16 = jnp.float32, jnp.bfloat16
    return pl.pallas_call(
        attention_kernel,
        out_shape=(jax.ShapeDtypeStruct((4, 2 * CHUNK, ROWS), bf16), tiles, tiles),
        in_specs=[pl.BlockSpec(memory_space=pltpu.SMEM)] + [vmem] * 4,
        out_specs=(vmem, vmem, vmem),
        scratch_shapes=[
            pltpu.VMEM((TILES, TILE, HEAD_SIZE), bf16),
            pltpu.VMEM((TILES, TILE, HEAD_SIZE), bf16),
            pltpu.VMEM((TILES, HEAD_SIZE, TILE), bf16),
            pltpu.VMEM((TILES, HEAD_SIZE, TILE), bf16),
            pltpu.VMEM((TILES, TILE, ROWS), f32),
            pltpu.VMEM((TILES, TILE, HEAD_SIZE), f32),
            pltpu.VMEM((TILES, TILE, HEAD_SIZE), f32),
            pltpu.VMEM((HEAD_SIZE, ROWS), f32),
            pltpu.VMEM((HEAD_SIZE, ROWS), f32),
            pltpu.VMEM((8, ROWS), f32),
            pltpu.VMEM((8, ROWS), f32),
        ],
        compiler_params=pltpu.CompilerParams(vmem_limit_bytes=48 << 20),
        cost_estimate=pl.CostEstimate(
            flops=4 * 10**9, bytes_accessed=6 << 20, transcendentals=3 * 10**6
        ),
        name="attention",
    )(scalars, begin, qd, kv_before, kv_own)


def per_device(queries, key_projection, value_projection, output_gradient, doc_lengths):
    z_hi = lax.axis_index("z_hi").astype(jnp.int32)
    block = lax.axis_index(BLOCK_AXES).astype(jnp.int32)
    anchor = (block - 1) * SPAN
    qd = lax.all_to_all(
        jnp.concatenate([queries, output_gradient], axis=0), "y", split_axis=1, concat_axis=0, tiled=True
    ).reshape(4, 2 * CHUNK, ROWS)
    kv = jnp.concatenate(
        [
            key_projection[:, :HEAD_SIZE], value_projection[:, :HEAD_SIZE],
            key_projection[:, HEAD_SIZE:], value_projection[:, HEAD_SIZE:],
        ],
        axis=1,
    )
    kv = lax.all_gather(kv, "z_hi", axis=0, tiled=True)
    first, second = kv[:, : 2 * HEAD_SIZE], kv[:, 2 * HEAD_SIZE :]
    kv_own = lax.all_to_all(
        jnp.stack([first, first, second, second]), "y", split_axis=0, concat_axis=0, tiled=True
    )
    blocks = lax.axis_size(BLOCK_AXES)
    kv_before = lax.ppermute(kv_own, BLOCK_AXES, [(i, i + 1) for i in range(blocks - 1)])
    docs = doc_lengths.shape[0]
    order = jnp.arange(docs)
    starts = jnp.sum(jnp.where(order[None, :] < order[:, None], doc_lengths[None, :], 0), axis=1)
    chunk_start = (4 * jnp.arange(4, dtype=jnp.int32) + z_hi) * CHUNK + anchor + SPAN
    position = (chunk_start[:, None] + jnp.arange(CHUNK, dtype=jnp.int32)[None, :])[..., None]
    begin = jnp.max(jnp.where(starts <= position, starts, 0), axis=2).astype(jnp.int32) - anchor
    scalars = jnp.concatenate([begin[:, 0] // TILE, z_hi[None]])
    begin = jnp.tile(begin, (1, HEADS)).reshape(4, 1, ROWS)

    shape = (OWN, TILE, 2 * HEAD_SIZE)
    out, grad_before, grad_own = attention(
        scalars, begin, qd, kv_before.reshape(shape), kv_own.reshape(shape)
    )
    returned = lax.ppermute(grad_before, BLOCK_AXES, [(i + 1, i) for i in range(blocks - 1)])
    grad_own = (grad_own.astype(jnp.float32) + returned.astype(jnp.float32)).astype(jnp.bfloat16)
    grad = lax.all_to_all(
        grad_own.reshape(4, 4, CHUNK, 2 * HEAD_SIZE), "y", split_axis=0, concat_axis=0, tiled=True
    ).astype(jnp.float32)
    grad = jnp.stack([grad[0] + grad[1], grad[2] + grad[3]], axis=1).astype(jnp.bfloat16)
    grad = lax.all_to_all(grad, "z_hi", split_axis=0, concat_axis=0, tiled=True)
    grad = jnp.sum(grad.astype(jnp.float32), axis=0).astype(jnp.bfloat16)
    keys_gradient = jnp.concatenate([grad[0, :, :HEAD_SIZE], grad[1, :, :HEAD_SIZE]], axis=1)
    values_gradient = jnp.concatenate([grad[0, :, HEAD_SIZE:], grad[1, :, HEAD_SIZE:]], axis=1)
    out = lax.all_to_all(
        out.reshape(4 * 2 * CHUNK, ROWS), "y", split_axis=0, concat_axis=1, tiled=True
    )
    return out[:CHUNK], out[CHUNK:], keys_gradient, values_gradient


def solution(mesh):
    order = [mesh.axis_names.index(name) for name in ("uly", "blk")]
    devices = np.transpose(mesh.devices, order).reshape(4, 4, 4, 4, 2)
    fine = Mesh(devices, ("y", "z_hi", "z_lo", "x", "core"))
    rows = P(TOKEN_AXES, None)
    return jax.shard_map(
        per_device, mesh=fine, in_specs=(rows, rows, rows, rows, P()),
        out_specs=(rows, rows, rows, rows), check_vma=False,
    )
```

```python
import math

import jax
import jax.numpy as jnp
import numpy as np
from jax import lax
from jax.experimental import pallas as pl
from jax.experimental.pallas import tpu as pltpu
from jax.sharding import Mesh
from jax.sharding import PartitionSpec as P

HEAD_SIZE = 128
SPAN = 2048
CHUNK = 128
TILE = 256
TILES = 2 * SPAN // TILE
OWN = SPAN // TILE
GROUP = 4
HEADS = 4
ROWS = HEADS * CHUNK
BLOCK_AXES = ("z_lo", "x", "core")
TOKEN_AXES = ("z_lo", "x", "core", "y", "z_hi")
SCALE = 1.0 / math.sqrt(HEAD_SIZE)
LOG2_SCALE = SCALE * math.log2(math.e)


def attention_kernel(
    scalars, begin_ref, qd_ref, kv_before_ref, kv_own_ref,
    out_ref, grad_before_ref, grad_own_ref,
    keys, values, keys_t, values_t, probs, grad_keys, grad_values, out_t, grad_query_t, top, total,
):
    z_hi = scalars[8]
    first = scalars[0]

    def load(source, shift):
        def body(tile, _):
            here = pl.ds(pl.multiple_of(tile * TILE, TILE), TILE)
            both = source[tile - shift]
            k, v = both[:, :HEAD_SIZE], both[:, HEAD_SIZE:]
            keys[here] = k
            values[here] = v
            keys_t[:, here] = k.T
            values_t[:, here] = v.T
            grad_keys[here] = jnp.zeros((TILE, HEAD_SIZE), jnp.float32)
            grad_values[here] = jnp.zeros((TILE, HEAD_SIZE), jnp.float32)
            return 0

        return body

    lax.fori_loop(first, OWN, load(kv_before_ref, 0), 0)
    lax.fori_loop(jnp.maximum(first, OWN), TILES, load(kv_own_ref, OWN), 0)

    def sweep(low, high, step):
        groups = (high - low) // GROUP
        lax.fori_loop(0, groups, lambda i, _: step(low + i * GROUP, GROUP), 0)
        if GROUP > 1:
            lax.fori_loop(low + groups * GROUP, high, lambda i, _: step(i, 1), 0)

    def chunk_step(chunk, _):
        start = SPAN + (4 * chunk + z_hi) * CHUNK
        low = scalars[chunk]
        high = (start + CHUNK - 1) // TILE + 1
        full_low = jnp.minimum((scalars[4 + chunk] + TILE - 1) // TILE, high)
        full_high = jnp.clip((start + 1) // TILE, full_low, high)
        block = qd_ref[chunk]
        rows_q = jnp.concatenate(
            [block[:CHUNK, h * HEAD_SIZE : (h + 1) * HEAD_SIZE] for h in range(HEADS)], axis=0
        )
        rows_d = jnp.concatenate(
            [block[CHUNK:, h * HEAD_SIZE : (h + 1) * HEAD_SIZE] for h in range(HEADS)], axis=0
        )
        query_pos = start + (lax.broadcasted_iota(jnp.int32, (1, ROWS), 1) & (CHUNK - 1))
        begin = begin_ref[chunk]
        top[...] = jnp.full((8, ROWS), -1e30, jnp.float32)
        total[...] = jnp.zeros((8, ROWS), jnp.float32)
        out_t[...] = jnp.zeros((HEAD_SIZE, ROWS), jnp.float32)
        grad_query_t[...] = jnp.zeros((HEAD_SIZE, ROWS), jnp.float32)

        def scores_step(masked):
            def step(tile, count):
                size = count * TILE
                here = pl.ds(pl.multiple_of(tile * TILE, TILE), size)
                s = LOG2_SCALE * lax.dot_general(
                    keys[here], rows_q, (((1,), (1,)), ((), ())), preferred_element_type=jnp.float32
                )
                if masked:
                    key_pos = tile * TILE + lax.broadcasted_iota(jnp.int32, (size, ROWS), 0)
                    allowed = (key_pos >= begin) & (key_pos <= query_pos)
                    s = jnp.where(allowed, s, -1e30)
                probs[here] = s
                top[...] = jnp.maximum(top[...], jnp.max(s.reshape(size // 8, 8, ROWS), axis=0))
                return 0

            return step

        sweep(low, full_low, scores_step(True))
        sweep(full_low, full_high, scores_step(False))
        sweep(full_high, high, scores_step(True))
        row_top = jnp.max(top[...], axis=0, keepdims=True)

        def output_step(tile, count):
            size = count * TILE
            here = pl.ds(pl.multiple_of(tile * TILE, TILE), size)
            p = jnp.exp2(probs[here] - row_top)
            probs[here] = p
            total[...] += jnp.sum(p.reshape(size // 8, 8, ROWS), axis=0)
            out_t[...] += lax.dot_general(
                values_t[:, here], p.astype(jnp.bfloat16), (((1,), (0,)), ((), ())),
                preferred_element_type=jnp.float32,
            )
            return 0

        sweep(low, high, output_step)
        inverse = 1.0 / jnp.sum(total[...], axis=0, keepdims=True)
        attended = out_t[...] * inverse
        context = attended.T
        delta = jnp.sum(rows_d.astype(jnp.float32).T * attended, axis=0, keepdims=True)

        def gradient_step(tile, count):
            size = count * TILE
            here = pl.ds(pl.multiple_of(tile * TILE, TILE), size)
            w = probs[here] * inverse
            grad_weights = lax.dot_general(
                values[here], rows_d, (((1,), (1,)), ((), ())), preferred_element_type=jnp.float32
            )
            grad_scores = (w * (grad_weights - delta)).astype(jnp.bfloat16)
            grad_values[here] += lax.dot_general(
                w.astype(jnp.bfloat16), rows_d, (((1,), (0,)), ((), ())),
                preferred_element_type=jnp.float32,
            )
            grad_keys[here] += lax.dot_general(
                grad_scores, rows_q, (((1,), (0,)), ((), ())), preferred_element_type=jnp.float32
            )
            grad_query_t[...] += lax.dot_general(
                keys_t[:, here], grad_scores, (((1,), (0,)), ((), ())),
                preferred_element_type=jnp.float32,
            )
            return 0

        sweep(low, high, gradient_step)
        grad_query = (grad_query_t[...] * SCALE).T
        for h in range(HEADS):
            span = slice(h * HEAD_SIZE, (h + 1) * HEAD_SIZE)
            out_ref[chunk, :CHUNK, span] = context[h * CHUNK : (h + 1) * CHUNK].astype(jnp.bfloat16)
            out_ref[chunk, CHUNK:, span] = grad_query[h * CHUNK : (h + 1) * CHUNK].astype(jnp.bfloat16)
        return 0

    lax.fori_loop(0, 4, chunk_step, 0)

    def store(target, shift):
        def body(tile, _):
            here = pl.ds(pl.multiple_of(tile * TILE, TILE), TILE)
            target[tile - shift, :, :HEAD_SIZE] = (grad_keys[here] * SCALE).astype(jnp.bfloat16)
            target[tile - shift, :, HEAD_SIZE:] = grad_values[here].astype(jnp.bfloat16)
            return 0

        return body

    def blank(target, shift):
        def body(tile, _):
            target[tile - shift] = jnp.zeros((TILE, 2 * HEAD_SIZE), jnp.bfloat16)
            return 0

        return body

    lax.fori_loop(0, jnp.minimum(first, OWN), blank(grad_before_ref, 0), 0)
    lax.fori_loop(OWN, first, blank(grad_own_ref, OWN), 0)
    lax.fori_loop(first, OWN, store(grad_before_ref, 0), 0)
    lax.fori_loop(jnp.maximum(first, OWN), TILES, store(grad_own_ref, OWN), 0)


def attention(scalars, begin, qd, kv_before, kv_own):
    vmem = pl.BlockSpec(memory_space=pltpu.VMEM)
    tiles = jax.ShapeDtypeStruct((OWN, TILE, 2 * HEAD_SIZE), jnp.bfloat16)
    f32, bf16 = jnp.float32, jnp.bfloat16
    return pl.pallas_call(
        attention_kernel,
        out_shape=(jax.ShapeDtypeStruct((4, 2 * CHUNK, ROWS), bf16), tiles, tiles),
        in_specs=[pl.BlockSpec(memory_space=pltpu.SMEM)] + [vmem] * 4,
        out_specs=(vmem, vmem, vmem),
        scratch_shapes=[
            pltpu.VMEM((2 * SPAN, HEAD_SIZE), bf16),
            pltpu.VMEM((2 * SPAN, HEAD_SIZE), bf16),
            pltpu.VMEM((HEAD_SIZE, 2 * SPAN), bf16),
            pltpu.VMEM((HEAD_SIZE, 2 * SPAN), bf16),
            pltpu.VMEM((2 * SPAN, ROWS), f32),
            pltpu.VMEM((2 * SPAN, HEAD_SIZE), f32),
            pltpu.VMEM((2 * SPAN, HEAD_SIZE), f32),
            pltpu.VMEM((HEAD_SIZE, ROWS), f32),
            pltpu.VMEM((HEAD_SIZE, ROWS), f32),
            pltpu.VMEM((8, ROWS), f32),
            pltpu.VMEM((8, ROWS), f32),
        ],
        compiler_params=pltpu.CompilerParams(vmem_limit_bytes=48 << 20),
        cost_estimate=pl.CostEstimate(
            flops=4 * 10**9, bytes_accessed=6 << 20, transcendentals=3 * 10**6
        ),
        name="attention",
    )(scalars, begin, qd, kv_before, kv_own)


def per_device(queries, key_projection, value_projection, output_gradient, doc_lengths):
    z_hi = lax.axis_index("z_hi").astype(jnp.int32)
    block = lax.axis_index(BLOCK_AXES).astype(jnp.int32)
    anchor = (block - 1) * SPAN
    qd = lax.all_to_all(
        jnp.concatenate([queries, output_gradient], axis=0), "y", split_axis=1, concat_axis=0, tiled=True
    ).reshape(4, 2 * CHUNK, ROWS)
    kv = jnp.concatenate(
        [
            key_projection[:, :HEAD_SIZE], value_projection[:, :HEAD_SIZE],
            key_projection[:, HEAD_SIZE:], value_projection[:, HEAD_SIZE:],
        ],
        axis=1,
    )
    kv = lax.all_gather(kv, "z_hi", axis=0, tiled=True)
    qd, kv = lax.optimization_barrier((qd, kv))
    first, second = kv[:, : 2 * HEAD_SIZE], kv[:, 2 * HEAD_SIZE :]
    kv_own = lax.all_to_all(
        jnp.stack([first, first, second, second]), "y", split_axis=0, concat_axis=0, tiled=True
    )
    blocks = lax.axis_size(BLOCK_AXES)
    kv_before = lax.ppermute(kv_own, BLOCK_AXES, [(i, i + 1) for i in range(blocks - 1)])
    docs = doc_lengths.shape[0]
    order = jnp.arange(docs)
    starts = jnp.sum(jnp.where(order[None, :] < order[:, None], doc_lengths[None, :], 0), axis=1)
    chunk_start = (4 * jnp.arange(4, dtype=jnp.int32) + z_hi) * CHUNK + anchor + SPAN
    position = (chunk_start[:, None] + jnp.arange(CHUNK, dtype=jnp.int32)[None, :])[..., None]
    begin = jnp.max(jnp.where(starts <= position, starts, 0), axis=2).astype(jnp.int32) - anchor
    scalars = jnp.concatenate([begin[:, 0] // TILE, begin[:, -1], z_hi[None]])
    begin = jnp.tile(begin, (1, HEADS)).reshape(4, 1, ROWS)

    shape = (OWN, TILE, 2 * HEAD_SIZE)
    out, grad_before, grad_own = attention(
        scalars, begin, qd, kv_before.reshape(shape), kv_own.reshape(shape)
    )
    returned = lax.ppermute(grad_before, BLOCK_AXES, [(i + 1, i) for i in range(blocks - 1)])
    out = lax.all_to_all(
        out.reshape(4 * 2 * CHUNK, ROWS), "y", split_axis=0, concat_axis=1, tiled=True
    )
    out, returned = lax.optimization_barrier((out, returned))
    grad_own = (grad_own.astype(jnp.float32) + returned.astype(jnp.float32)).astype(jnp.bfloat16)
    grad = lax.all_to_all(
        grad_own.reshape(4, 4, CHUNK, 2 * HEAD_SIZE), "y", split_axis=0, concat_axis=0, tiled=True
    ).astype(jnp.float32)
    grad = jnp.stack([grad[0] + grad[1], grad[2] + grad[3]], axis=1).astype(jnp.bfloat16)
    grad = lax.all_to_all(grad, "z_hi", split_axis=0, concat_axis=0, tiled=True)
    grad = jnp.sum(grad.astype(jnp.float32), axis=0).astype(jnp.bfloat16)
    keys_gradient = jnp.concatenate([grad[0, :, :HEAD_SIZE], grad[1, :, :HEAD_SIZE]], axis=1)
    values_gradient = jnp.concatenate([grad[0, :, HEAD_SIZE:], grad[1, :, HEAD_SIZE:]], axis=1)
    return out[:CHUNK], out[CHUNK:], keys_gradient, values_gradient


def solution(mesh):
    order = [mesh.axis_names.index(name) for name in ("uly", "blk")]
    devices = np.transpose(mesh.devices, order).reshape(4, 4, 4, 4, 2)
    fine = Mesh(devices, ("y", "z_hi", "z_lo", "x", "core"))
    rows = P(TOKEN_AXES, None)
    return jax.shard_map(
        per_device, mesh=fine, in_specs=(rows, rows, rows, rows, P()),
        out_specs=(rows, rows, rows, rows), check_vma=False,
    )
```

```python
import math

import jax
import jax.numpy as jnp
import numpy as np
from jax import lax
from jax.experimental import pallas as pl
from jax.experimental.pallas import tpu as pltpu
from jax.sharding import Mesh
from jax.sharding import PartitionSpec as P

HEAD_SIZE = 128
SPAN = 2048
CHUNK = 128
TILE = 256
TILES = SPAN // TILE
GROUP = 4
BACK_GROUP = 2
HEADS = 4
ROWS = HEADS * CHUNK
BLOCK_AXES = ("z_lo", "x", "core")
TOKEN_AXES = ("z_lo", "x", "core", "y", "z_hi")
SCALE = 1.0 / math.sqrt(HEAD_SIZE)
LOG2_SCALE = SCALE * math.log2(math.e)
F32, BF16 = jnp.float32, jnp.bfloat16


def dot(a, b, contract):
    return lax.dot_general(a, b, (contract, ((), ())), preferred_element_type=F32)


def rows_of(ref, chunk, part):
    block = ref[chunk, part * CHUNK : (part + 1) * CHUNK]
    return jnp.concatenate(
        [block[:, h * HEAD_SIZE : (h + 1) * HEAD_SIZE] for h in range(HEADS)], axis=0
    )


def store_rows(ref, chunk, value):
    for h in range(HEADS):
        ref[chunk, :, h * HEAD_SIZE : (h + 1) * HEAD_SIZE] = value[
            h * CHUNK : (h + 1) * CHUNK
        ].astype(BF16)


def at(tile, count=1):
    return pl.ds(pl.multiple_of(tile * TILE, TILE), count * TILE)


def sweep(low, high, step, group):
    groups = (high - low) // group

    def many(i, _):
        step(low + i * group, group)
        return 0

    def one(i, _):
        step(i, 1)
        return 0

    lax.fori_loop(0, groups, many, 0)
    if group > 1:
        lax.fori_loop(low + groups * group, high, one, 0)


def own_range(scalars, chunk):
    start = (4 * chunk + scalars[8]) * CHUNK
    low = jnp.maximum(scalars[chunk], 0) // TILE
    high = (start + CHUNK - 1) // TILE + 1
    full_low = jnp.minimum((jnp.maximum(scalars[4 + chunk], 0) + TILE - 1) // TILE, high)
    full_high = jnp.clip((start + 1) // TILE, full_low, high)
    return start, low, high, full_low, full_high


def before_range(scalars, chunk):
    low = jnp.minimum(scalars[chunk] + SPAN, SPAN) // TILE
    full_low = jnp.minimum((scalars[4 + chunk] + SPAN + TILE - 1) // TILE, TILES)
    return low, full_low


def position_in_rows(start):
    return start + (lax.broadcasted_iota(jnp.int32, (1, ROWS), 1) & (CHUNK - 1))


def scores(keys, rows_q, tile, count, limits):
    s = LOG2_SCALE * dot(keys, rows_q, ((1,), (1,)))
    if limits is not None:
        begin, last = limits
        key_pos = tile * TILE + lax.broadcasted_iota(jnp.int32, (count * TILE, ROWS), 0)
        allowed = key_pos >= begin
        if last is not None:
            allowed &= key_pos <= last
        s = jnp.where(allowed, s, -1e30)
    return s


def fold(value, how):
    return how(value.reshape(value.shape[0] // 8, 8, ROWS), axis=0)


def own_forward(scalars, begin_ref, qd_ref, kv_ref, stats_ref, out_ref, values_t, probs, top, total):
    first = jnp.maximum(scalars[0], 0) // TILE

    def load(tile, _):
        values_t[:, at(tile)] = kv_ref[at(tile), HEAD_SIZE:].T
        return 0

    lax.fori_loop(first, TILES, load, 0)

    def chunk_step(chunk, _):
        start, low, high, full_low, full_high = own_range(scalars, chunk)
        rows_q = rows_of(qd_ref, chunk, 0)
        limits = (begin_ref[chunk], position_in_rows(start))
        top[...] = jnp.full((8, ROWS), -1e30, F32)
        total[...] = jnp.zeros((8, ROWS), F32)
        out_ref[chunk] = jnp.zeros((HEAD_SIZE, ROWS), F32)

        def scores_step(limits):
            def step(tile, count):
                here = at(tile, count)
                s = scores(kv_ref[here, :HEAD_SIZE], rows_q, tile, count, limits)
                probs[here] = s
                top[...] = jnp.maximum(top[...], fold(s, jnp.max))

            return step

        sweep(low, full_low, scores_step(limits), GROUP)
        sweep(full_low, full_high, scores_step(None), GROUP)
        sweep(full_high, high, scores_step(limits), GROUP)
        row_top = jnp.max(top[...], axis=0, keepdims=True)

        def output_step(tile, count):
            here = at(tile, count)
            p = jnp.exp2(probs[here] - row_top)
            total[...] += fold(p, jnp.sum)
            out_ref[chunk] += dot(values_t[:, here], p.astype(BF16), ((1,), (0,)))

        sweep(low, high, output_step, GROUP)
        stats_ref[chunk, 0:1] = row_top
        stats_ref[chunk, 1:2] = jnp.sum(total[...], axis=0, keepdims=True)
        return 0

    lax.fori_loop(0, 4, chunk_step, 0)


def before_part(
    scalars, begin_ref, qd_ref, kv_ref, stats_in, out_in,
    context_ref, grad_ref, stats_ref, grad_query_ref,
    keys_t, values_t, probs, grad_keys, grad_values, out_t, top, total,
):
    first = jnp.minimum(scalars[0] + SPAN, SPAN) // TILE

    def load(tile, _):
        keys_t[:, at(tile)] = kv_ref[at(tile), :HEAD_SIZE].T
        values_t[:, at(tile)] = kv_ref[at(tile), HEAD_SIZE:].T
        grad_keys[at(tile)] = jnp.zeros((TILE, HEAD_SIZE), F32)
        grad_values[at(tile)] = jnp.zeros((TILE, HEAD_SIZE), F32)
        return 0

    lax.fori_loop(first, TILES, load, 0)

    def blank(tile, _):
        grad_ref[at(tile)] = jnp.zeros((TILE, 2 * HEAD_SIZE), BF16)
        return 0

    lax.fori_loop(0, first, blank, 0)

    def chunk_step(chunk, _):
        low, full_low = before_range(scalars, chunk)
        rows_q = rows_of(qd_ref, chunk, 0)
        rows_d = rows_of(qd_ref, chunk, 1)
        limits = (begin_ref[chunk] + SPAN, None)
        own_top, own_total = stats_in[chunk, 0:1], stats_in[chunk, 1:2]
        top[...] = jnp.broadcast_to(own_top, (8, ROWS))
        total[...] = jnp.zeros((8, ROWS), F32)
        grad_query_ref[chunk] = jnp.zeros((HEAD_SIZE, ROWS), F32)

        def scores_step(limits):
            def step(tile, count):
                here = at(tile, count)
                s = scores(kv_ref[here, :HEAD_SIZE], rows_q, tile, count, limits)
                probs[here] = s
                top[...] = jnp.maximum(top[...], fold(s, jnp.max))

            return step

        sweep(low, full_low, scores_step(limits), GROUP)
        sweep(full_low, TILES, scores_step(None), GROUP)
        row_top = jnp.max(top[...], axis=0, keepdims=True)
        rescale = jnp.exp2(own_top - row_top)
        out_t[...] = out_in[chunk] * rescale

        def output_step(tile, count):
            here = at(tile, count)
            p = jnp.exp2(probs[here] - row_top)
            probs[here] = p
            total[...] += fold(p, jnp.sum)
            out_t[...] += dot(values_t[:, here], p.astype(BF16), ((1,), (0,)))

        sweep(low, TILES, output_step, GROUP)
        row_total = jnp.sum(total[...], axis=0, keepdims=True) + own_total * rescale
        inverse = 1.0 / row_total
        attended = out_t[...] * inverse
        delta = jnp.sum(rows_d.astype(F32).T * attended, axis=0, keepdims=True)
        store_rows(context_ref, chunk, attended.T)
        stats_ref[chunk, 0:1] = row_top + jnp.log2(row_total)
        stats_ref[chunk, 1:2] = delta

        def gradient_step(tile, count):
            here = at(tile, count)
            w = probs[here] * inverse
            grad_weights = dot(kv_ref[here, HEAD_SIZE:], rows_d, ((1,), (1,)))
            grad_scores = (w * (grad_weights - delta)).astype(BF16)
            grad_values[here] += dot(w.astype(BF16), rows_d, ((1,), (0,)))
            grad_keys[here] += dot(grad_scores, rows_q, ((1,), (0,)))
            grad_query_ref[chunk] += dot(keys_t[:, here], grad_scores, ((1,), (0,)))

        sweep(low, TILES, gradient_step, GROUP)
        return 0

    lax.fori_loop(0, 4, chunk_step, 0)

    def store(tile, _):
        grad_ref[at(tile), :HEAD_SIZE] = (grad_keys[at(tile)] * SCALE).astype(BF16)
        grad_ref[at(tile), HEAD_SIZE:] = grad_values[at(tile)].astype(BF16)
        return 0

    lax.fori_loop(first, TILES, store, 0)


def own_backward(
    scalars, begin_ref, qd_ref, kv_ref, stats_in, grad_query_in,
    grad_query_ref, grad_ref, keys_t, grad_keys, grad_values, grad_query_t,
):
    first = jnp.maximum(scalars[0], 0) // TILE

    def load(tile, _):
        keys_t[:, at(tile)] = kv_ref[at(tile), :HEAD_SIZE].T
        grad_keys[at(tile)] = jnp.zeros((TILE, HEAD_SIZE), F32)
        grad_values[at(tile)] = jnp.zeros((TILE, HEAD_SIZE), F32)
        return 0

    lax.fori_loop(first, TILES, load, 0)

    def blank(tile, _):
        grad_ref[at(tile)] = jnp.zeros((TILE, 2 * HEAD_SIZE), BF16)
        return 0

    lax.fori_loop(0, first, blank, 0)

    def chunk_step(chunk, _):
        start, low, high, full_low, full_high = own_range(scalars, chunk)
        rows_q = rows_of(qd_ref, chunk, 0)
        rows_d = rows_of(qd_ref, chunk, 1)
        limits = (begin_ref[chunk], position_in_rows(start))
        log_total, delta = stats_in[chunk, 0:1], stats_in[chunk, 1:2]
        grad_query_t[...] = grad_query_in[chunk]

        def gradient_step(limits):
            def step(tile, count):
                here = at(tile, count)
                s = scores(kv_ref[here, :HEAD_SIZE], rows_q, tile, count, limits)
                w = jnp.exp2(s - log_total)
                grad_weights = dot(kv_ref[here, HEAD_SIZE:], rows_d, ((1,), (1,)))
                grad_scores = (w * (grad_weights - delta)).astype(BF16)
                grad_values[here] += dot(w.astype(BF16), rows_d, ((1,), (0,)))
                grad_keys[here] += dot(grad_scores, rows_q, ((1,), (0,)))
                grad_query_t[...] += dot(keys_t[:, here], grad_scores, ((1,), (0,)))

            return step

        sweep(low, full_low, gradient_step(limits), BACK_GROUP)
        sweep(full_low, full_high, gradient_step(None), BACK_GROUP)
        sweep(full_high, high, gradient_step(limits), BACK_GROUP)
        store_rows(grad_query_ref, chunk, (grad_query_t[...] * SCALE).T)
        return 0

    lax.fori_loop(0, 4, chunk_step, 0)

    def store(tile, _):
        grad_ref[at(tile), :HEAD_SIZE] = (grad_keys[at(tile)] * SCALE).astype(BF16)
        grad_ref[at(tile), HEAD_SIZE:] = grad_values[at(tile)].astype(BF16)
        return 0

    lax.fori_loop(first, TILES, store, 0)


def call(kernel, name, gflops, outs, scratch, *args):
    vmem = pl.BlockSpec(memory_space=pltpu.VMEM)
    return pl.pallas_call(
        kernel,
        out_shape=tuple(jax.ShapeDtypeStruct(shape, dtype) for shape, dtype in outs),
        in_specs=[pl.BlockSpec(memory_space=pltpu.SMEM)] + [vmem] * (len(args) - 1),
        out_specs=tuple(vmem for _ in outs),
        scratch_shapes=[pltpu.VMEM(shape, dtype) for shape, dtype in scratch],
        compiler_params=pltpu.CompilerParams(vmem_limit_bytes=36 << 20),
        cost_estimate=pl.CostEstimate(
            flops=gflops * 10**9, bytes_accessed=4 << 20, transcendentals=2 * 10**6
        ),
        name=name,
    )(*args)


STATS = ((4, 2, ROWS), F32)
ACROSS = ((4, HEAD_SIZE, ROWS), F32)
RESULT = ((4, CHUNK, ROWS), BF16)
GRADS = ((SPAN, 2 * HEAD_SIZE), BF16)
TURNED = ((HEAD_SIZE, SPAN), BF16)
SQUARE = ((SPAN, ROWS), F32)
SUMS = ((SPAN, HEAD_SIZE), F32)
FLAT = ((HEAD_SIZE, ROWS), F32)
EIGHT = ((8, ROWS), F32)


def run_own_forward(scalars, begin, qd, kv):
    return call(
        own_forward, "own_forward", 2, (STATS, ACROSS), (TURNED, SQUARE, EIGHT, EIGHT),
        scalars, begin, qd, kv,
    )


def run_before_part(scalars, begin, qd, kv, stats, out):
    return call(
        before_part, "before_part", 2, (RESULT, GRADS, STATS, ACROSS),
        (TURNED, TURNED, SQUARE, SUMS, SUMS, FLAT, EIGHT, EIGHT),
        scalars, begin, qd, kv, stats, out,
    )


def run_own_backward(scalars, begin, qd, kv, stats, grad_query):
    return call(
        own_backward, "own_backward", 3, (RESULT, GRADS), (TURNED, SUMS, SUMS, FLAT),
        scalars, begin, qd, kv, stats, grad_query,
    )


def columns(value, index, count):
    width = value.shape[1] // count
    return value[:, index * width : (index + 1) * width]


def per_device(queries, key_projection, value_projection, output_gradient, doc_lengths):
    z_hi = lax.axis_index("z_hi").astype(jnp.int32)
    block = lax.axis_index(BLOCK_AXES).astype(jnp.int32)
    blocks = lax.axis_size(BLOCK_AXES)
    own_start = block * SPAN
    qd = jnp.stack(
        [
            jnp.concatenate([columns(queries, d, 4), columns(output_gradient, d, 4)], axis=0)
            for d in range(4)
        ]
    )
    qd = lax.all_to_all(qd, "y", split_axis=0, concat_axis=0, tiled=True)
    kv = jnp.concatenate(
        [
            columns(part, head, 2)
            for head in range(2)
            for part in (key_projection, value_projection)
        ],
        axis=1,
    )
    kv = lax.all_gather(kv, "z_hi", axis=0, tiled=True)
    qd, kv = lax.optimization_barrier((qd, kv))
    first, second = columns(kv, 0, 2), columns(kv, 1, 2)
    kv_own = lax.all_to_all(
        jnp.stack([first, first, second, second]), "y", split_axis=0, concat_axis=0, tiled=True
    ).reshape(SPAN, 2 * HEAD_SIZE)
    kv_before = lax.ppermute(kv_own, BLOCK_AXES, [(i, i + 1) for i in range(blocks - 1)])
    docs = doc_lengths.shape[0]
    order = jnp.arange(docs)
    starts = jnp.sum(jnp.where(order[None, :] < order[:, None], doc_lengths[None, :], 0), axis=1)
    chunk_start = (4 * jnp.arange(4, dtype=jnp.int32) + z_hi) * CHUNK + own_start
    position = (chunk_start[:, None] + jnp.arange(CHUNK, dtype=jnp.int32)[None, :])[..., None]
    begin = jnp.max(jnp.where(starts <= position, starts, 0), axis=2).astype(jnp.int32) - own_start
    scalars = jnp.concatenate([begin[:, 0], begin[:, -1], z_hi[None]])
    begin = jnp.tile(begin, (1, HEADS)).reshape(4, 1, ROWS)

    stats, out = run_own_forward(scalars, begin, qd, kv_own)
    kv_before, stats, out = lax.optimization_barrier((kv_before, stats, out))
    context, grad_before, stats, grad_query = run_before_part(
        scalars, begin, qd, kv_before, stats, out
    )
    returned = lax.ppermute(grad_before, BLOCK_AXES, [(i + 1, i) for i in range(blocks - 1)])
    context = lax.all_to_all(context, "y", split_axis=0, concat_axis=0, tiled=True)
    grad_query, grad_own = run_own_backward(scalars, begin, qd, kv_own, stats, grad_query)
    context, returned, grad_own = lax.optimization_barrier((context, returned, grad_own))
    grad_own = (grad_own.astype(F32) + returned.astype(F32)).astype(BF16)
    grad = lax.all_to_all(
        grad_own.reshape(4, 4, CHUNK, 2 * HEAD_SIZE), "y", split_axis=0, concat_axis=0, tiled=True
    )

    def part(step):
        mine = lax.dynamic_index_in_dim(grad, (z_hi + step) % 4, axis=1, keepdims=False).astype(F32)
        return jnp.stack([mine[0] + mine[1], mine[2] + mine[3]])

    arrived = [
        lax.ppermute(part(step).astype(BF16), "z_hi", [(i, (i + step) % 4) for i in range(4)])
        for step in (2, 1, 3)
    ]
    grad_query = lax.all_to_all(grad_query, "y", split_axis=0, concat_axis=0, tiled=True)
    grad_query, *arrived = lax.optimization_barrier((grad_query, *arrived))
    grad = part(0)
    for piece in arrived:
        grad += piece.astype(F32)
    grad = grad.astype(BF16)
    keys_gradient = jnp.concatenate([grad[0, :, :HEAD_SIZE], grad[1, :, :HEAD_SIZE]], axis=1)
    values_gradient = jnp.concatenate([grad[0, :, HEAD_SIZE:], grad[1, :, HEAD_SIZE:]], axis=1)
    return (
        jnp.concatenate([context[i] for i in range(4)], axis=1),
        jnp.concatenate([grad_query[i] for i in range(4)], axis=1),
        keys_gradient,
        values_gradient,
    )


def solution(mesh):
    order = [mesh.axis_names.index(name) for name in ("uly", "blk")]
    devices = np.transpose(mesh.devices, order).reshape(4, 4, 4, 4, 2)
    fine = Mesh(devices, ("y", "z_hi", "z_lo", "x", "core"))
    rows = P(TOKEN_AXES, None)
    return jax.shard_map(
        per_device, mesh=fine, in_specs=(rows, rows, rows, rows, P()),
        out_specs=(rows, rows, rows, rows), check_vma=False,
    )
```

```python
import math

import jax
import jax.numpy as jnp
import numpy as np
from jax import lax
from jax.experimental import pallas as pl
from jax.experimental.pallas import tpu as pltpu
from jax.sharding import Mesh
from jax.sharding import PartitionSpec as P

HEAD_SIZE = 128
SPAN = 2048
CHUNK = 128
TILE = 256
TILES = SPAN // TILE
GROUP = 4
BACK_GROUP = 2
HEADS = 4
ROWS = HEADS * CHUNK
BLOCK_AXES = ("z_lo", "x", "core")
TOKEN_AXES = ("z_lo", "x", "core", "y", "z_hi")
SCALE = 1.0 / math.sqrt(HEAD_SIZE)
LOG2_SCALE = SCALE * math.log2(math.e)
F32, BF16 = jnp.float32, jnp.bfloat16


def dot(a, b, contract):
    return lax.dot_general(a, b, (contract, ((), ())), preferred_element_type=F32)


def rows_of(ref, chunk, part):
    block = ref[chunk, part * CHUNK : (part + 1) * CHUNK]
    return jnp.concatenate(
        [block[:, h * HEAD_SIZE : (h + 1) * HEAD_SIZE] for h in range(HEADS)], axis=0
    )


def store_rows(ref, chunk, value):
    for h in range(HEADS):
        ref[chunk, :, h * HEAD_SIZE : (h + 1) * HEAD_SIZE] = value[
            h * CHUNK : (h + 1) * CHUNK
        ].astype(BF16)


def at(tile, count=1):
    return pl.ds(pl.multiple_of(tile * TILE, TILE), count * TILE)


def sweep(low, high, step, group):
    groups = (high - low) // group

    def many(i, _):
        step(low + i * group, group)
        return 0

    def one(i, _):
        step(i, 1)
        return 0

    lax.fori_loop(0, groups, many, 0)
    if group > 1:
        lax.fori_loop(low + groups * group, high, one, 0)


def own_range(scalars, chunk):
    start = (4 * chunk + scalars[8]) * CHUNK
    low = jnp.maximum(scalars[chunk], 0) // TILE
    high = (start + CHUNK - 1) // TILE + 1
    full_low = jnp.minimum((jnp.maximum(scalars[4 + chunk], 0) + TILE - 1) // TILE, high)
    full_high = jnp.clip((start + 1) // TILE, full_low, high)
    return start, low, high, full_low, full_high


def before_range(scalars, chunk):
    low = jnp.minimum(scalars[chunk] + SPAN, SPAN) // TILE
    full_low = jnp.minimum((scalars[4 + chunk] + SPAN + TILE - 1) // TILE, TILES)
    return low, full_low


def position_in_rows(start):
    return start + (lax.broadcasted_iota(jnp.int32, (1, ROWS), 1) & (CHUNK - 1))


def scores(keys, rows_q, tile, count, limits):
    s = LOG2_SCALE * dot(keys, rows_q, ((1,), (1,)))
    if limits is not None:
        begin, last = limits
        key_pos = tile * TILE + lax.broadcasted_iota(jnp.int32, (count * TILE, ROWS), 0)
        allowed = key_pos >= begin
        if last is not None:
            allowed &= key_pos <= last
        s = jnp.where(allowed, s, -1e30)
    return s


def fold(value, how):
    return how(value.reshape(value.shape[0] // 8, 8, ROWS), axis=0)


def own_forward(scalars, begin_ref, qd_ref, kv_ref, stats_ref, out_ref, values_t, probs, top, total):
    first = jnp.maximum(scalars[0], 0) // TILE

    def load(tile, _):
        values_t[:, at(tile)] = kv_ref[at(tile), HEAD_SIZE:].T
        return 0

    lax.fori_loop(first, TILES, load, 0)

    def chunk_step(chunk, _):
        start, low, high, full_low, full_high = own_range(scalars, chunk)
        rows_q = rows_of(qd_ref, chunk, 0)
        limits = (begin_ref[chunk], position_in_rows(start))
        top[...] = jnp.full((8, ROWS), -1e30, F32)
        total[...] = jnp.zeros((8, ROWS), F32)
        out_ref[chunk] = jnp.zeros((HEAD_SIZE, ROWS), F32)

        def scores_step(limits):
            def step(tile, count):
                here = at(tile, count)
                s = scores(kv_ref[here, :HEAD_SIZE], rows_q, tile, count, limits)
                probs[here] = s
                top[...] = jnp.maximum(top[...], fold(s, jnp.max))

            return step

        sweep(low, full_low, scores_step(limits), GROUP)
        sweep(full_low, full_high, scores_step(None), GROUP)
        sweep(full_high, high, scores_step(limits), GROUP)
        row_top = jnp.max(top[...], axis=0, keepdims=True)

        def output_step(tile, count):
            here = at(tile, count)
            p = jnp.exp2(probs[here] - row_top)
            total[...] += fold(p, jnp.sum)
            out_ref[chunk] += dot(values_t[:, here], p.astype(BF16), ((1,), (0,)))

        sweep(low, high, output_step, GROUP)
        stats_ref[chunk, 0:1] = row_top
        stats_ref[chunk, 1:2] = jnp.sum(total[...], axis=0, keepdims=True)
        return 0

    lax.fori_loop(0, 4, chunk_step, 0)


def before_part(
    scalars, begin_ref, qd_ref, kv_ref, stats_in, out_in,
    context_ref, grad_ref, stats_ref, grad_query_ref,
    keys_t, values_t, probs, grad_keys, grad_values, out_t, top, total,
):
    first = jnp.minimum(scalars[0] + SPAN, SPAN) // TILE

    def load(tile, _):
        keys_t[:, at(tile)] = kv_ref[at(tile), :HEAD_SIZE].T
        values_t[:, at(tile)] = kv_ref[at(tile), HEAD_SIZE:].T
        grad_keys[at(tile)] = jnp.zeros((TILE, HEAD_SIZE), F32)
        grad_values[at(tile)] = jnp.zeros((TILE, HEAD_SIZE), F32)
        return 0

    lax.fori_loop(first, TILES, load, 0)

    def blank(tile, _):
        grad_ref[at(tile)] = jnp.zeros((TILE, 2 * HEAD_SIZE), BF16)
        return 0

    lax.fori_loop(0, first, blank, 0)

    def chunk_step(chunk, _):
        low, full_low = before_range(scalars, chunk)
        rows_q = rows_of(qd_ref, chunk, 0)
        rows_d = rows_of(qd_ref, chunk, 1)
        limits = (begin_ref[chunk] + SPAN, None)
        own_top, own_total = stats_in[chunk, 0:1], stats_in[chunk, 1:2]
        top[...] = jnp.broadcast_to(own_top, (8, ROWS))
        total[...] = jnp.zeros((8, ROWS), F32)
        grad_query_ref[chunk] = jnp.zeros((HEAD_SIZE, ROWS), F32)

        def scores_step(limits):
            def step(tile, count):
                here = at(tile, count)
                s = scores(kv_ref[here, :HEAD_SIZE], rows_q, tile, count, limits)
                probs[here] = s
                top[...] = jnp.maximum(top[...], fold(s, jnp.max))

            return step

        sweep(low, full_low, scores_step(limits), GROUP)
        sweep(full_low, TILES, scores_step(None), GROUP)
        row_top = jnp.max(top[...], axis=0, keepdims=True)
        rescale = jnp.exp2(own_top - row_top)
        out_t[...] = out_in[chunk] * rescale

        def output_step(tile, count):
            here = at(tile, count)
            p = jnp.exp2(probs[here] - row_top)
            probs[here] = p
            total[...] += fold(p, jnp.sum)
            out_t[...] += dot(values_t[:, here], p.astype(BF16), ((1,), (0,)))

        sweep(low, TILES, output_step, GROUP)
        row_total = jnp.sum(total[...], axis=0, keepdims=True) + own_total * rescale
        inverse = 1.0 / row_total
        attended = out_t[...] * inverse
        delta = jnp.sum(rows_d.astype(F32).T * attended, axis=0, keepdims=True)
        store_rows(context_ref, chunk, attended.T)
        stats_ref[chunk, 0:1] = row_top + jnp.log2(row_total)
        stats_ref[chunk, 1:2] = delta

        def gradient_step(tile, count):
            here = at(tile, count)
            w = probs[here] * inverse
            grad_weights = dot(kv_ref[here, HEAD_SIZE:], rows_d, ((1,), (1,)))
            grad_scores = (w * (grad_weights - delta)).astype(BF16)
            grad_values[here] += dot(w.astype(BF16), rows_d, ((1,), (0,)))
            grad_keys[here] += dot(grad_scores, rows_q, ((1,), (0,)))
            grad_query_ref[chunk] += dot(keys_t[:, here], grad_scores, ((1,), (0,)))

        sweep(low, TILES, gradient_step, GROUP)
        return 0

    lax.fori_loop(0, 4, chunk_step, 0)

    def store(tile, _):
        grad_ref[at(tile), :HEAD_SIZE] = (grad_keys[at(tile)] * SCALE).astype(BF16)
        grad_ref[at(tile), HEAD_SIZE:] = grad_values[at(tile)].astype(BF16)
        return 0

    lax.fori_loop(first, TILES, store, 0)


def own_backward(
    scalars, begin_ref, qd_ref, kv_ref, stats_in, grad_query_in,
    grad_query_ref, grad_ref, keys_t, grad_keys, grad_values, grad_query_t,
):
    first = jnp.maximum(scalars[0], 0) // TILE

    def load(tile, _):
        keys_t[:, at(tile)] = kv_ref[at(tile), :HEAD_SIZE].T
        grad_keys[at(tile)] = jnp.zeros((TILE, HEAD_SIZE), F32)
        grad_values[at(tile)] = jnp.zeros((TILE, HEAD_SIZE), F32)
        return 0

    lax.fori_loop(first, TILES, load, 0)

    def blank(tile, _):
        grad_ref[at(tile)] = jnp.zeros((TILE, 2 * HEAD_SIZE), BF16)
        return 0

    lax.fori_loop(0, first, blank, 0)

    def chunk_step(chunk, _):
        start, low, high, full_low, full_high = own_range(scalars, chunk)
        rows_q = rows_of(qd_ref, chunk, 0)
        rows_d = rows_of(qd_ref, chunk, 1)
        limits = (begin_ref[chunk], position_in_rows(start))
        log_total, delta = stats_in[chunk, 0:1], stats_in[chunk, 1:2]
        grad_query_t[...] = grad_query_in[chunk]

        def gradient_step(limits):
            def step(tile, count):
                here = at(tile, count)
                s = scores(kv_ref[here, :HEAD_SIZE], rows_q, tile, count, limits)
                w = jnp.exp2(s - log_total)
                grad_weights = dot(kv_ref[here, HEAD_SIZE:], rows_d, ((1,), (1,)))
                grad_scores = (w * (grad_weights - delta)).astype(BF16)
                grad_values[here] += dot(w.astype(BF16), rows_d, ((1,), (0,)))
                grad_keys[here] += dot(grad_scores, rows_q, ((1,), (0,)))
                grad_query_t[...] += dot(keys_t[:, here], grad_scores, ((1,), (0,)))

            return step

        sweep(low, full_low, gradient_step(limits), BACK_GROUP)
        sweep(full_low, full_high, gradient_step(None), BACK_GROUP)
        sweep(full_high, high, gradient_step(limits), BACK_GROUP)
        store_rows(grad_query_ref, (chunk - scalars[9]) & 3, (grad_query_t[...] * SCALE).T)
        return 0

    lax.fori_loop(0, 4, chunk_step, 0)

    def store(tile, _):
        grad_ref[at(tile), :HEAD_SIZE] = (grad_keys[at(tile)] * SCALE).astype(BF16)
        grad_ref[at(tile), HEAD_SIZE:] = grad_values[at(tile)].astype(BF16)
        return 0

    lax.fori_loop(first, TILES, store, 0)


def call(kernel, name, gflops, megabytes, outs, scratch, *args):
    vmem = pl.BlockSpec(memory_space=pltpu.VMEM)
    return pl.pallas_call(
        kernel,
        out_shape=tuple(jax.ShapeDtypeStruct(shape, dtype) for shape, dtype in outs),
        in_specs=[pl.BlockSpec(memory_space=pltpu.SMEM)] + [vmem] * (len(args) - 1),
        out_specs=tuple(vmem for _ in outs),
        scratch_shapes=[pltpu.VMEM(shape, dtype) for shape, dtype in scratch],
        compiler_params=pltpu.CompilerParams(vmem_limit_bytes=megabytes << 20),
        cost_estimate=pl.CostEstimate(
            flops=gflops * 10**9, bytes_accessed=4 << 20, transcendentals=2 * 10**6
        ),
        name=name,
    )(*args)


STATS = ((4, 2, ROWS), F32)
ACROSS = ((4, HEAD_SIZE, ROWS), F32)
RESULT = ((4, CHUNK, ROWS), BF16)
GRADS = ((SPAN, 2 * HEAD_SIZE), BF16)
TURNED = ((HEAD_SIZE, SPAN), BF16)
SQUARE = ((SPAN, ROWS), F32)
SUMS = ((SPAN, HEAD_SIZE), F32)
FLAT = ((HEAD_SIZE, ROWS), F32)
EIGHT = ((8, ROWS), F32)


def run_own_forward(scalars, begin, qd, kv):
    return call(
        own_forward, "own_forward", 2, 12, (STATS, ACROSS), (TURNED, SQUARE, EIGHT, EIGHT),
        scalars, begin, qd, kv,
    )


def run_before_part(scalars, begin, qd, kv, stats, out):
    return call(
        before_part, "before_part", 2, 18, (RESULT, GRADS, STATS, ACROSS),
        (TURNED, TURNED, SQUARE, SUMS, SUMS, FLAT, EIGHT, EIGHT),
        scalars, begin, qd, kv, stats, out,
    )


def run_own_backward(scalars, begin, qd, kv, stats, grad_query):
    return call(
        own_backward, "own_backward", 3, 14, (RESULT, GRADS), (TURNED, SUMS, SUMS, FLAT),
        scalars, begin, qd, kv, stats, grad_query,
    )


def small(kernel, name, outs, scalar, *args):
    vmem = pl.BlockSpec(memory_space=pltpu.VMEM)
    smem = [pl.BlockSpec(memory_space=pltpu.SMEM)] if scalar is not None else []
    return pl.pallas_call(
        kernel,
        out_shape=tuple(jax.ShapeDtypeStruct(shape, dtype) for shape, dtype in outs),
        in_specs=smem + [vmem] * len(args),
        out_specs=tuple(vmem for _ in outs),
        compiler_params=pltpu.CompilerParams(vmem_limit_bytes=8 << 20),
        cost_estimate=pl.CostEstimate(flops=10**6, bytes_accessed=2 << 20, transcendentals=0),
        name=name,
    )(*([scalar] if scalar is not None else []), *args)


def pack(queries, output_gradient, keys, values):
    def kernel(q_ref, d_ref, k_ref, v_ref, qd_ref, kv_ref):
        for d in range(4):
            span = slice(d * ROWS, (d + 1) * ROWS)
            qd_ref[d, :CHUNK] = q_ref[:, span]
            qd_ref[d, CHUNK:] = d_ref[:, span]
        for head in range(2):
            here = slice(head * HEAD_SIZE, (head + 1) * HEAD_SIZE)
            kv_ref[:, 2 * head * HEAD_SIZE : (2 * head + 1) * HEAD_SIZE] = k_ref[:, here]
            kv_ref[:, (2 * head + 1) * HEAD_SIZE : (2 * head + 2) * HEAD_SIZE] = v_ref[:, here]

    outs = (((4, 2 * CHUNK, ROWS), BF16), ((CHUNK, 4 * HEAD_SIZE), BF16))
    return small(kernel, "pack", outs, None, queries, output_gradient, keys, values)


def join(y, *pieces):
    def kernel(y_ref, *refs):
        out = refs[-1]
        for step in range(4):
            group = (y_ref[0] - step) & 3
            out[:, pl.ds(pl.multiple_of(group * ROWS, ROWS), ROWS)] = refs[step][...]

    return small(kernel, "join", (((CHUNK, 4 * ROWS), BF16),), y, *pieces)[0]


def last_sum(grad):
    def kernel(grad_ref, keys_ref, values_ref):
        for head in range(2):
            total = sum(grad_ref[i, head].astype(F32) for i in range(4)).astype(BF16)
            here = slice(head * HEAD_SIZE, (head + 1) * HEAD_SIZE)
            keys_ref[:, here] = total[:, :HEAD_SIZE]
            values_ref[:, here] = total[:, HEAD_SIZE:]

    outs = (((CHUNK, 2 * HEAD_SIZE), BF16),) * 2
    return small(kernel, "last_sum", outs, None, grad)


def columns(value, index, count):
    width = value.shape[1] // count
    return value[:, index * width : (index + 1) * width]


def per_device(queries, key_projection, value_projection, output_gradient, doc_lengths):
    z_hi = lax.axis_index("z_hi").astype(jnp.int32)
    y = lax.axis_index("y").astype(jnp.int32)
    block = lax.axis_index(BLOCK_AXES).astype(jnp.int32)
    blocks = lax.axis_size(BLOCK_AXES)
    own_start = block * SPAN
    qd, kv = pack(queries, output_gradient, key_projection, value_projection)
    qd = lax.all_to_all(qd, "y", split_axis=0, concat_axis=0, tiled=True)
    kv = lax.all_gather(kv, "z_hi", axis=0, tiled=True)
    qd, kv = lax.optimization_barrier((qd, kv))
    first, second = columns(kv, 0, 2), columns(kv, 1, 2)
    kv_own = lax.all_to_all(
        jnp.stack([first, first, second, second]), "y", split_axis=0, concat_axis=0, tiled=True
    ).reshape(SPAN, 2 * HEAD_SIZE)
    kv_before = lax.ppermute(kv_own, BLOCK_AXES, [(i, i + 1) for i in range(blocks - 1)])
    docs = doc_lengths.shape[0]
    order = jnp.arange(docs)
    starts = jnp.sum(jnp.where(order[None, :] < order[:, None], doc_lengths[None, :], 0), axis=1)
    chunk_start = (4 * jnp.arange(4, dtype=jnp.int32) + z_hi) * CHUNK + own_start
    position = (chunk_start[:, None] + jnp.arange(CHUNK, dtype=jnp.int32)[None, :])[..., None]
    begin = jnp.max(jnp.where(starts <= position, starts, 0), axis=2).astype(jnp.int32) - own_start
    scalars = jnp.concatenate([begin[:, 0], begin[:, -1], z_hi[None], y[None]])
    begin = jnp.tile(begin, (1, HEADS)).reshape(4, 1, ROWS)

    stats, out = run_own_forward(scalars, begin, qd, kv_own)
    kv_before, stats, out = lax.optimization_barrier((kv_before, stats, out))
    context, grad_before, stats, grad_query = run_before_part(
        scalars, begin, qd, kv_before, stats, out
    )
    returned = lax.ppermute(grad_before, BLOCK_AXES, [(i + 1, i) for i in range(blocks - 1)])
    context = lax.all_to_all(context, "y", split_axis=0, concat_axis=0, tiled=True)
    grad_query, grad_own = run_own_backward(scalars, begin, qd, kv_own, stats, grad_query)
    context, returned, grad_own = lax.optimization_barrier((context, returned, grad_own))
    grad_own = (grad_own.astype(F32) + returned.astype(F32)).astype(BF16)
    grad = lax.all_to_all(
        grad_own.reshape(4, 4, CHUNK, 2 * HEAD_SIZE), "y", split_axis=0, concat_axis=0, tiled=True
    )

    grad = grad.astype(F32)
    grad = jnp.stack([grad[0] + grad[1], grad[2] + grad[3]], axis=1).astype(BF16)
    grad, grad_query = lax.optimization_barrier((grad, grad_query))
    grad = lax.all_to_all(grad, "z_hi", split_axis=0, concat_axis=0, tiled=True)
    pieces = [grad_query[0]] + [
        lax.ppermute(grad_query[step], "y", [(i, (i + step) % 4) for i in range(4)])
        for step in (1, 2, 3)
    ]
    grad_queries = join(y[None], *pieces)
    keys_gradient, values_gradient = last_sum(grad)
    return (
        jnp.concatenate([context[i] for i in range(4)], axis=1),
        grad_queries,
        keys_gradient,
        values_gradient,
    )


def solution(mesh):
    order = [mesh.axis_names.index(name) for name in ("uly", "blk")]
    devices = np.transpose(mesh.devices, order).reshape(4, 4, 4, 4, 2)
    fine = Mesh(devices, ("y", "z_hi", "z_lo", "x", "core"))
    rows = P(TOKEN_AXES, None)
    return jax.shard_map(
        per_device, mesh=fine, in_specs=(rows, rows, rows, rows, P()),
        out_specs=(rows, rows, rows, rows), check_vma=False,
    )
```

```python
import math

import jax
import jax.numpy as jnp
import numpy as np
from jax import lax
from jax.experimental import pallas as pl
from jax.experimental.pallas import tpu as pltpu
from jax.sharding import Mesh
from jax.sharding import PartitionSpec as P

HEAD_SIZE = 128
SPAN = 2048
CHUNK = 128
TILE = 256
TILES = SPAN // TILE
GROUP = 4
BACK_GROUP = 2
HEADS = 4
ROWS = HEADS * CHUNK
BLOCK_AXES = ("z_lo", "x", "core")
TOKEN_AXES = ("z_lo", "x", "core", "y", "z_hi")
SCALE = 1.0 / math.sqrt(HEAD_SIZE)
LOG2_SCALE = SCALE * math.log2(math.e)
F32, BF16 = jnp.float32, jnp.bfloat16


def dot(a, b, contract):
    return lax.dot_general(a, b, (contract, ((), ())), preferred_element_type=F32)


def rows_of(ref, chunk, part):
    block = ref[chunk, part * CHUNK : (part + 1) * CHUNK]
    return jnp.concatenate(
        [block[:, h * HEAD_SIZE : (h + 1) * HEAD_SIZE] for h in range(HEADS)], axis=0
    )


def store_rows(ref, chunk, value):
    for h in range(HEADS):
        ref[chunk, :, h * HEAD_SIZE : (h + 1) * HEAD_SIZE] = value[
            h * CHUNK : (h + 1) * CHUNK
        ].astype(BF16)


def at(tile, count=1):
    return pl.ds(pl.multiple_of(tile * TILE, TILE), count * TILE)


def sweep(low, high, step, group):
    groups = (high - low) // group

    def many(i, _):
        step(low + i * group, group)
        return 0

    def one(i, _):
        step(i, 1)
        return 0

    lax.fori_loop(0, groups, many, 0)
    if group > 1:
        lax.fori_loop(low + groups * group, high, one, 0)


def own_range(scalars, chunk):
    start = (4 * chunk + scalars[8]) * CHUNK
    low = jnp.maximum(scalars[chunk], 0) // TILE
    high = (start + CHUNK - 1) // TILE + 1
    full_low = jnp.minimum((jnp.maximum(scalars[4 + chunk], 0) + TILE - 1) // TILE, high)
    full_high = jnp.clip((start + 1) // TILE, full_low, high)
    return start, low, high, full_low, full_high


def before_range(scalars, chunk):
    low = jnp.minimum(scalars[chunk] + SPAN, SPAN) // TILE
    full_low = jnp.minimum((scalars[4 + chunk] + SPAN + TILE - 1) // TILE, TILES)
    return low, full_low


def position_in_rows(start):
    return start + (lax.broadcasted_iota(jnp.int32, (1, ROWS), 1) & (CHUNK - 1))


def scores(keys, rows_q, tile, count, limits):
    s = LOG2_SCALE * dot(keys, rows_q, ((1,), (1,)))
    if limits is not None:
        begin, last = limits
        key_pos = tile * TILE + lax.broadcasted_iota(jnp.int32, (count * TILE, ROWS), 0)
        allowed = key_pos >= begin
        if last is not None:
            allowed &= key_pos <= last
        s = jnp.where(allowed, s, -1e30)
    return s


def fold(value, how):
    return how(value.reshape(value.shape[0] // 8, 8, ROWS), axis=0)


def own_forward(scalars, begin_ref, qd_ref, kv_ref, stats_ref, out_ref, values_t, probs, top, total):
    first = jnp.maximum(scalars[0], 0) // TILE

    def load(tile, _):
        values_t[:, at(tile)] = kv_ref[at(tile), HEAD_SIZE:].T
        return 0

    lax.fori_loop(first, TILES, load, 0)

    def chunk_step(chunk, _):
        start, low, high, full_low, full_high = own_range(scalars, chunk)
        rows_q = rows_of(qd_ref, chunk, 0)
        limits = (begin_ref[chunk], position_in_rows(start))
        top[...] = jnp.full((8, ROWS), -1e30, F32)
        total[...] = jnp.zeros((8, ROWS), F32)
        out_ref[chunk] = jnp.zeros((HEAD_SIZE, ROWS), F32)

        def scores_step(limits):
            def step(tile, count):
                here = at(tile, count)
                s = scores(kv_ref[here, :HEAD_SIZE], rows_q, tile, count, limits)
                probs[here] = s
                top[...] = jnp.maximum(top[...], fold(s, jnp.max))

            return step

        sweep(low, full_low, scores_step(limits), GROUP)
        sweep(full_low, full_high, scores_step(None), GROUP)
        sweep(full_high, high, scores_step(limits), GROUP)
        row_top = jnp.max(top[...], axis=0, keepdims=True)

        def output_step(tile, count):
            here = at(tile, count)
            p = jnp.exp2(probs[here] - row_top)
            total[...] += fold(p, jnp.sum)
            out_ref[chunk] += dot(values_t[:, here], p.astype(BF16), ((1,), (0,)))

        sweep(low, high, output_step, GROUP)
        stats_ref[chunk, 0:1] = row_top
        stats_ref[chunk, 1:2] = jnp.sum(total[...], axis=0, keepdims=True)
        return 0

    lax.fori_loop(0, 4, chunk_step, 0)


def before_part(
    scalars, begin_ref, qd_ref, kv_ref, stats_in, out_in,
    context_ref, grad_ref, stats_ref, grad_query_ref,
    keys_t, values_t, probs, grad_keys, grad_values, out_t, grad_query, top, total, sem,
):
    first = jnp.minimum(scalars[0] + SPAN, SPAN) // TILE

    def load(tile, _):
        keys_t[:, at(tile)] = kv_ref[at(tile), :HEAD_SIZE].T
        values_t[:, at(tile)] = kv_ref[at(tile), HEAD_SIZE:].T
        grad_keys[at(tile)] = jnp.zeros((TILE, HEAD_SIZE), F32)
        grad_values[at(tile)] = jnp.zeros((TILE, HEAD_SIZE), F32)
        return 0

    lax.fori_loop(first, TILES, load, 0)

    def blank(tile, _):
        grad_ref[at(tile)] = jnp.zeros((TILE, 2 * HEAD_SIZE), BF16)
        return 0

    lax.fori_loop(0, first, blank, 0)

    def hand_over(chunk):
        return pltpu.make_async_copy(
            grad_query.at[chunk], grad_query_ref.at[chunk], sem.at[chunk]
        )

    def chunk_step(chunk, _):
        low, full_low = before_range(scalars, chunk)
        rows_q = rows_of(qd_ref, chunk, 0)
        rows_d = rows_of(qd_ref, chunk, 1)
        limits = (begin_ref[chunk] + SPAN, None)
        own_top, own_total = stats_in[chunk, 0:1], stats_in[chunk, 1:2]
        top[...] = jnp.broadcast_to(own_top, (8, ROWS))
        total[...] = jnp.zeros((8, ROWS), F32)
        grad_query[chunk] = jnp.zeros((HEAD_SIZE, ROWS), F32)

        def scores_step(limits):
            def step(tile, count):
                here = at(tile, count)
                s = scores(kv_ref[here, :HEAD_SIZE], rows_q, tile, count, limits)
                probs[here] = s
                top[...] = jnp.maximum(top[...], fold(s, jnp.max))

            return step

        sweep(low, full_low, scores_step(limits), GROUP)
        sweep(full_low, TILES, scores_step(None), GROUP)
        row_top = jnp.max(top[...], axis=0, keepdims=True)
        rescale = jnp.exp2(own_top - row_top)
        out_t[...] = out_in[chunk] * rescale

        def output_step(tile, count):
            here = at(tile, count)
            p = jnp.exp2(probs[here] - row_top)
            probs[here] = p
            total[...] += fold(p, jnp.sum)
            out_t[...] += dot(values_t[:, here], p.astype(BF16), ((1,), (0,)))

        sweep(low, TILES, output_step, GROUP)
        row_total = jnp.sum(total[...], axis=0, keepdims=True) + own_total * rescale
        inverse = 1.0 / row_total
        attended = out_t[...] * inverse
        delta = jnp.sum(rows_d.astype(F32).T * attended, axis=0, keepdims=True)
        store_rows(context_ref, chunk, attended.T)
        stats_ref[chunk, 0:1] = row_top + jnp.log2(row_total)
        stats_ref[chunk, 1:2] = delta

        def gradient_step(tile, count):
            here = at(tile, count)
            w = probs[here] * inverse
            grad_weights = dot(kv_ref[here, HEAD_SIZE:], rows_d, ((1,), (1,)))
            grad_scores = (w * (grad_weights - delta)).astype(BF16)
            grad_values[here] += dot(w.astype(BF16), rows_d, ((1,), (0,)))
            grad_keys[here] += dot(grad_scores, rows_q, ((1,), (0,)))
            grad_query[chunk] += dot(keys_t[:, here], grad_scores, ((1,), (0,)))

        sweep(low, TILES, gradient_step, GROUP)
        hand_over(chunk).start()
        return 0

    lax.fori_loop(0, 4, chunk_step, 0)

    def store(tile, _):
        grad_ref[at(tile), :HEAD_SIZE] = (grad_keys[at(tile)] * SCALE).astype(BF16)
        grad_ref[at(tile), HEAD_SIZE:] = grad_values[at(tile)].astype(BF16)
        return 0

    lax.fori_loop(first, TILES, store, 0)
    for chunk in range(4):
        hand_over(chunk).wait()


def own_backward(
    scalars, begin_ref, qd_ref, kv_ref, stats_in, grad_query_in,
    out_0, out_1, out_2, out_3, grad_ref,
    keys_t, grad_keys, grad_values, grad_query_t, grad_query, sem,
):
    first = jnp.maximum(scalars[0], 0) // TILE

    def fetch(chunk):
        return pltpu.make_async_copy(
            grad_query_in.at[chunk], grad_query_t.at[chunk], sem.at[chunk]
        )

    for chunk in range(4):
        fetch(chunk).start()

    def load(tile, _):
        keys_t[:, at(tile)] = kv_ref[at(tile), :HEAD_SIZE].T
        grad_keys[at(tile)] = jnp.zeros((TILE, HEAD_SIZE), F32)
        grad_values[at(tile)] = jnp.zeros((TILE, HEAD_SIZE), F32)
        return 0

    lax.fori_loop(first, TILES, load, 0)

    def blank(tile, _):
        grad_ref[at(tile)] = jnp.zeros((TILE, 2 * HEAD_SIZE), BF16)
        return 0

    lax.fori_loop(0, first, blank, 0)

    def chunk_step(chunk, _):
        start, low, high, full_low, full_high = own_range(scalars, chunk)
        rows_q = rows_of(qd_ref, chunk, 0)
        rows_d = rows_of(qd_ref, chunk, 1)
        limits = (begin_ref[chunk], position_in_rows(start))
        log_total, delta = stats_in[chunk, 0:1], stats_in[chunk, 1:2]
        fetch(chunk).wait()

        def gradient_step(limits):
            def step(tile, count):
                here = at(tile, count)
                s = scores(kv_ref[here, :HEAD_SIZE], rows_q, tile, count, limits)
                w = jnp.exp2(s - log_total)
                grad_weights = dot(kv_ref[here, HEAD_SIZE:], rows_d, ((1,), (1,)))
                grad_scores = (w * (grad_weights - delta)).astype(BF16)
                grad_values[here] += dot(w.astype(BF16), rows_d, ((1,), (0,)))
                grad_keys[here] += dot(grad_scores, rows_q, ((1,), (0,)))
                grad_query_t[chunk] += dot(keys_t[:, here], grad_scores, ((1,), (0,)))

            return step

        sweep(low, full_low, gradient_step(limits), BACK_GROUP)
        sweep(full_low, full_high, gradient_step(None), BACK_GROUP)
        sweep(full_high, high, gradient_step(limits), BACK_GROUP)
        store_rows(grad_query, (chunk - scalars[9]) & 3, (grad_query_t[chunk] * SCALE).T)
        return 0

    lax.fori_loop(0, 4, chunk_step, 0)

    def store(tile, _):
        grad_ref[at(tile), :HEAD_SIZE] = (grad_keys[at(tile)] * SCALE).astype(BF16)
        grad_ref[at(tile), HEAD_SIZE:] = grad_values[at(tile)].astype(BF16)
        return 0

    lax.fori_loop(first, TILES, store, 0)
    for slot, out in enumerate((out_0, out_1, out_2, out_3)):
        out[...] = grad_query[slot]


def call(kernel, name, gflops, megabytes, outs, scratch, *args, hbm_in=(), hbm_out=(), sems=0):
    vmem, hbm = pl.BlockSpec(memory_space=pltpu.VMEM), pl.BlockSpec(memory_space=pltpu.HBM)
    return pl.pallas_call(
        kernel,
        out_shape=tuple(jax.ShapeDtypeStruct(shape, dtype) for shape, dtype in outs),
        in_specs=[pl.BlockSpec(memory_space=pltpu.SMEM)]
        + [hbm if n in hbm_in else vmem for n in range(1, len(args))],
        out_specs=tuple(hbm if n in hbm_out else vmem for n in range(len(outs))),
        scratch_shapes=[pltpu.VMEM(shape, dtype) for shape, dtype in scratch]
        + ([pltpu.SemaphoreType.DMA((sems,))] if sems else []),
        compiler_params=pltpu.CompilerParams(vmem_limit_bytes=megabytes << 20),
        cost_estimate=pl.CostEstimate(
            flops=gflops * 10**9, bytes_accessed=4 << 20, transcendentals=2 * 10**6
        ),
        name=name,
    )(*args)


STATS = ((4, 2, ROWS), F32)
ACROSS = ((4, HEAD_SIZE, ROWS), F32)
RESULT = ((4, CHUNK, ROWS), BF16)
PIECE = ((CHUNK, ROWS), BF16)
GRADS = ((SPAN, 2 * HEAD_SIZE), BF16)
TURNED = ((HEAD_SIZE, SPAN), BF16)
SQUARE = ((SPAN, ROWS), F32)
SUMS = ((SPAN, HEAD_SIZE), F32)
FLAT = ((HEAD_SIZE, ROWS), F32)
EIGHT = ((8, ROWS), F32)


def run_own_forward(scalars, begin, qd, kv):
    return call(
        own_forward, "own_forward", 2, 12, (STATS, ACROSS), (TURNED, SQUARE, EIGHT, EIGHT),
        scalars, begin, qd, kv,
    )


def run_before_part(scalars, begin, qd, kv, stats, out):
    return call(
        before_part, "before_part", 2, 18, (RESULT, GRADS, STATS, ACROSS),
        (TURNED, TURNED, SQUARE, SUMS, SUMS, FLAT, ACROSS, EIGHT, EIGHT),
        scalars, begin, qd, kv, stats, out, hbm_out=(3,), sems=4,
    )


def run_own_backward(scalars, begin, qd, kv, stats, grad_query):
    return call(
        own_backward, "own_backward", 3, 60, (PIECE,) * 4 + (GRADS,),
        (TURNED, SUMS, SUMS, ACROSS, RESULT), scalars, begin, qd, kv, stats, grad_query,
        hbm_in=(5,), sems=4,
    )


def small(kernel, name, outs, scalar, *args):
    vmem = pl.BlockSpec(memory_space=pltpu.VMEM)
    smem = [pl.BlockSpec(memory_space=pltpu.SMEM)] if scalar is not None else []
    return pl.pallas_call(
        kernel,
        out_shape=tuple(jax.ShapeDtypeStruct(shape, dtype) for shape, dtype in outs),
        in_specs=smem + [vmem] * len(args),
        out_specs=tuple(vmem for _ in outs),
        compiler_params=pltpu.CompilerParams(vmem_limit_bytes=8 << 20),
        cost_estimate=pl.CostEstimate(flops=10**6, bytes_accessed=2 << 20, transcendentals=0),
        name=name,
    )(*([scalar] if scalar is not None else []), *args)


def pack(queries, output_gradient, keys, values):
    def kernel(q_ref, d_ref, k_ref, v_ref, qd_ref, kv_ref, sem):
        moves = []
        for index, source in enumerate((k_ref, v_ref)):
            for head in range(2):
                slot = 2 * head + index
                moves.append(
                    (
                        source.at[:, pl.ds(head * HEAD_SIZE, HEAD_SIZE)],
                        kv_ref.at[:, pl.ds(slot * HEAD_SIZE, HEAD_SIZE)],
                    )
                )
        for index, source in enumerate((q_ref, d_ref)):
            for d in range(4):
                moves.append(
                    (
                        source.at[:, pl.ds(d * ROWS, ROWS)],
                        qd_ref.at[d, pl.ds(index * CHUNK, CHUNK)],
                    )
                )
        copies = [
            pltpu.make_async_copy(source, target, sem.at[n])
            for n, (source, target) in enumerate(moves)
        ]
        for copy in copies:
            copy.start()
        for copy in copies:
            copy.wait()

    hbm = pl.BlockSpec(memory_space=pltpu.HBM)
    return pl.pallas_call(
        kernel,
        out_shape=(
            jax.ShapeDtypeStruct((4, 2 * CHUNK, ROWS), BF16),
            jax.ShapeDtypeStruct((CHUNK, 4 * HEAD_SIZE), BF16),
        ),
        in_specs=[hbm] * 4,
        out_specs=(hbm, hbm),
        scratch_shapes=[pltpu.SemaphoreType.DMA((12,))],
        compiler_params=pltpu.CompilerParams(vmem_limit_bytes=60 << 20),
        cost_estimate=pl.CostEstimate(flops=10**6, bytes_accessed=2 << 20, transcendentals=0),
        name="pack",
    )(queries, output_gradient, keys, values)


def join(y, *pieces):
    def kernel(y_ref, *refs):
        out = refs[-1]
        for step in range(4):
            group = (y_ref[0] - step) & 3
            out[:, pl.ds(pl.multiple_of(group * ROWS, ROWS), ROWS)] = refs[step][...]

    return small(kernel, "join", (((CHUNK, 4 * ROWS), BF16),), y, *pieces)[0]


def last_sum(grad):
    def kernel(grad_ref, keys_ref, values_ref):
        for head in range(2):
            total = sum(grad_ref[i, head].astype(F32) for i in range(4)).astype(BF16)
            here = slice(head * HEAD_SIZE, (head + 1) * HEAD_SIZE)
            keys_ref[:, here] = total[:, :HEAD_SIZE]
            values_ref[:, here] = total[:, HEAD_SIZE:]

    outs = (((CHUNK, 2 * HEAD_SIZE), BF16),) * 2
    return small(kernel, "last_sum", outs, None, grad)


def columns(value, index, count):
    width = value.shape[1] // count
    return value[:, index * width : (index + 1) * width]


def per_device(queries, key_projection, value_projection, output_gradient, doc_lengths):
    z_hi = lax.axis_index("z_hi").astype(jnp.int32)
    y = lax.axis_index("y").astype(jnp.int32)
    block = lax.axis_index(BLOCK_AXES).astype(jnp.int32)
    blocks = lax.axis_size(BLOCK_AXES)
    own_start = block * SPAN
    qd, kv = pack(queries, output_gradient, key_projection, value_projection)
    qd = lax.all_to_all(qd, "y", split_axis=0, concat_axis=0, tiled=True)
    kv = lax.all_gather(kv, "z_hi", axis=0, tiled=True)
    qd, kv = lax.optimization_barrier((qd, kv))
    first, second = columns(kv, 0, 2), columns(kv, 1, 2)
    kv_own = lax.all_to_all(
        jnp.stack([first, first, second, second]), "y", split_axis=0, concat_axis=0, tiled=True
    ).reshape(SPAN, 2 * HEAD_SIZE)
    kv_before = lax.ppermute(kv_own, BLOCK_AXES, [(i, i + 1) for i in range(blocks - 1)])
    docs = doc_lengths.shape[0]
    order = jnp.arange(docs)
    starts = jnp.sum(jnp.where(order[None, :] < order[:, None], doc_lengths[None, :], 0), axis=1)
    chunk_start = (4 * jnp.arange(4, dtype=jnp.int32) + z_hi) * CHUNK + own_start
    position = (chunk_start[:, None] + jnp.arange(CHUNK, dtype=jnp.int32)[None, :])[..., None]
    begin = jnp.max(jnp.where(starts <= position, starts, 0), axis=2).astype(jnp.int32) - own_start
    scalars = jnp.concatenate([begin[:, 0], begin[:, -1], z_hi[None], y[None]])
    begin = jnp.tile(begin, (1, HEADS)).reshape(4, 1, ROWS)

    stats, out = run_own_forward(scalars, begin, qd, kv_own)
    kv_before, stats, out = lax.optimization_barrier((kv_before, stats, out))
    context, grad_before, stats, grad_query = run_before_part(
        scalars, begin, qd, kv_before, stats, out
    )
    returned = lax.ppermute(grad_before, BLOCK_AXES, [(i + 1, i) for i in range(blocks - 1)])
    context = lax.all_to_all(context, "y", split_axis=0, concat_axis=0, tiled=True)
    *grad_query, grad_own = run_own_backward(scalars, begin, qd, kv_own, stats, grad_query)
    context, returned, grad_own = lax.optimization_barrier((context, returned, grad_own))
    grad_own = (grad_own.astype(F32) + returned.astype(F32)).astype(BF16)
    grad = lax.all_to_all(
        grad_own.reshape(4, 4, CHUNK, 2 * HEAD_SIZE), "y", split_axis=0, concat_axis=0, tiled=True
    )

    grad = grad.astype(F32)
    grad = jnp.stack([grad[0] + grad[1], grad[2] + grad[3]], axis=1).astype(BF16)
    grad, *grad_query = lax.optimization_barrier((grad, *grad_query))
    grad = lax.all_to_all(grad, "z_hi", split_axis=0, concat_axis=0, tiled=True)
    pieces = [grad_query[0]] + [
        lax.ppermute(grad_query[step], "y", [(i, (i + step) % 4) for i in range(4)])
        for step in (1, 2, 3)
    ]
    grad_queries = join(y[None], *pieces)
    keys_gradient, values_gradient = last_sum(grad)
    return (
        jnp.concatenate([context[i] for i in range(4)], axis=1),
        grad_queries,
        keys_gradient,
        values_gradient,
    )


def solution(mesh):
    order = [mesh.axis_names.index(name) for name in ("uly", "blk")]
    devices = np.transpose(mesh.devices, order).reshape(4, 4, 4, 4, 2)
    fine = Mesh(devices, ("y", "z_hi", "z_lo", "x", "core"))
    rows = P(TOKEN_AXES, None)
    return jax.shard_map(
        per_device, mesh=fine, in_specs=(rows, rows, rows, rows, P()),
        out_specs=(rows, rows, rows, rows), check_vma=False,
    )
```

```python
import math

import jax
import jax.numpy as jnp
import numpy as np
from jax import lax
from jax.experimental import pallas as pl
from jax.experimental.pallas import tpu as pltpu
from jax.sharding import Mesh
from jax.sharding import PartitionSpec as P

HEAD_SIZE = 128
SPAN = 2048
CHUNK = 128
TILE = 256
TILES = SPAN // TILE
GROUP = 4
BACK_GROUP = 2
HEADS = 4
ROWS = HEADS * CHUNK
BLOCK_AXES = ("z_lo", "x", "core")
TOKEN_AXES = ("z_lo", "x", "core", "y", "z_hi")
SCALE = 1.0 / math.sqrt(HEAD_SIZE)
LOG2_SCALE = SCALE * math.log2(math.e)
F32, BF16 = jnp.float32, jnp.bfloat16


def dot(a, b, contract):
    return lax.dot_general(a, b, (contract, ((), ())), preferred_element_type=F32)


def rows_of(ref, chunk, part):
    block = ref[chunk, part * CHUNK : (part + 1) * CHUNK]
    return jnp.concatenate(
        [block[:, h * HEAD_SIZE : (h + 1) * HEAD_SIZE] for h in range(HEADS)], axis=0
    )


def store_rows(ref, chunk, value):
    for h in range(HEADS):
        ref[chunk, :, h * HEAD_SIZE : (h + 1) * HEAD_SIZE] = value[
            h * CHUNK : (h + 1) * CHUNK
        ].astype(BF16)


def at(tile, count=1):
    return pl.ds(pl.multiple_of(tile * TILE, TILE), count * TILE)


def sweep(low, high, step, group):
    groups = (high - low) // group

    def many(i, _):
        step(low + i * group, group)
        return 0

    def one(i, _):
        step(i, 1)
        return 0

    lax.fori_loop(0, groups, many, 0)
    if group > 1:
        lax.fori_loop(low + groups * group, high, one, 0)


def own_range(scalars, chunk):
    start = (4 * chunk + scalars[8]) * CHUNK
    low = jnp.maximum(scalars[chunk], 0) // TILE
    high = (start + CHUNK - 1) // TILE + 1
    full_low = jnp.minimum((jnp.maximum(scalars[4 + chunk], 0) + TILE - 1) // TILE, high)
    full_high = jnp.clip((start + 1) // TILE, full_low, high)
    return start, low, high, full_low, full_high


def before_range(scalars, chunk):
    low = jnp.minimum(scalars[chunk] + SPAN, SPAN) // TILE
    full_low = jnp.minimum((scalars[4 + chunk] + SPAN + TILE - 1) // TILE, TILES)
    return low, full_low


def position_in_rows(start):
    return start + (lax.broadcasted_iota(jnp.int32, (1, ROWS), 1) & (CHUNK - 1))


def load_halves(scalars, first, mine_ref, other_ref, keep):
    half = TILES // 2
    for ref, which in ((mine_ref, scalars[9] & 1), (other_ref, 1 - (scalars[9] & 1))):
        shift = which * half

        def body(tile, _, ref=ref, shift=shift):
            both = ref[at(tile - shift)]
            keep(tile, both[:, :HEAD_SIZE], both[:, HEAD_SIZE:])
            return 0

        lax.fori_loop(jnp.maximum(first, shift), shift + half, body, 0)


def scores(keys, rows_q, tile, count, limits):
    s = LOG2_SCALE * dot(keys, rows_q, ((1,), (1,)))
    if limits is not None:
        begin, last = limits
        key_pos = tile * TILE + lax.broadcasted_iota(jnp.int32, (count * TILE, ROWS), 0)
        allowed = key_pos >= begin
        if last is not None:
            allowed &= key_pos <= last
        s = jnp.where(allowed, s, -1e30)
    return s


def fold(value, how):
    return how(value.reshape(value.shape[0] // 8, 8, ROWS), axis=0)


def own_forward(
    scalars, begin_ref, qd_ref, mine_ref, other_ref,
    stats_ref, out_ref, keys, values_t, probs, top, total,
):
    first = jnp.maximum(scalars[0], 0) // TILE

    def keep(tile, k, v):
        keys[at(tile)] = k
        values_t[:, at(tile)] = v.T

    load_halves(scalars, first, mine_ref, other_ref, keep)

    def chunk_step(chunk, _):
        start, low, high, full_low, full_high = own_range(scalars, chunk)
        rows_q = rows_of(qd_ref, chunk, 0)
        limits = (begin_ref[chunk], position_in_rows(start))
        top[...] = jnp.full((8, ROWS), -1e30, F32)
        total[...] = jnp.zeros((8, ROWS), F32)
        out_ref[chunk] = jnp.zeros((HEAD_SIZE, ROWS), F32)

        def scores_step(limits):
            def step(tile, count):
                here = at(tile, count)
                s = scores(keys[here], rows_q, tile, count, limits)
                probs[here] = s
                top[...] = jnp.maximum(top[...], fold(s, jnp.max))

            return step

        sweep(low, full_low, scores_step(limits), GROUP)
        sweep(full_low, full_high, scores_step(None), GROUP)
        sweep(full_high, high, scores_step(limits), GROUP)
        row_top = jnp.max(top[...], axis=0, keepdims=True)

        def output_step(tile, count):
            here = at(tile, count)
            p = jnp.exp2(probs[here] - row_top)
            total[...] += fold(p, jnp.sum)
            out_ref[chunk] += dot(values_t[:, here], p.astype(BF16), ((1,), (0,)))

        sweep(low, high, output_step, GROUP)
        stats_ref[chunk, 0:1] = row_top
        stats_ref[chunk, 1:2] = jnp.sum(total[...], axis=0, keepdims=True)
        return 0

    lax.fori_loop(0, 4, chunk_step, 0)


def before_part(
    scalars, begin_ref, qd_ref, mine_ref, other_ref, stats_in, out_in,
    context_ref, grad_ref, stats_ref, grad_query_ref, keys, values,
    keys_t, values_t, probs, grad_keys, grad_values, out_t, grad_query, top, total, sem,
):
    first = jnp.minimum(scalars[0] + SPAN, SPAN) // TILE

    def keep(tile, k, v):
        keys[at(tile)] = k
        values[at(tile)] = v
        keys_t[:, at(tile)] = k.T
        values_t[:, at(tile)] = v.T
        grad_keys[at(tile)] = jnp.zeros((TILE, HEAD_SIZE), F32)
        grad_values[at(tile)] = jnp.zeros((TILE, HEAD_SIZE), F32)

    load_halves(scalars, first, mine_ref, other_ref, keep)

    def blank(tile, _):
        grad_ref[at(tile)] = jnp.zeros((TILE, 2 * HEAD_SIZE), BF16)
        return 0

    lax.fori_loop(0, first, blank, 0)

    def hand_over(chunk):
        return pltpu.make_async_copy(
            grad_query.at[chunk], grad_query_ref.at[chunk], sem.at[chunk]
        )

    def chunk_step(chunk, _):
        low, full_low = before_range(scalars, chunk)
        rows_q = rows_of(qd_ref, chunk, 0)
        rows_d = rows_of(qd_ref, chunk, 1)
        limits = (begin_ref[chunk] + SPAN, None)
        own_top, own_total = stats_in[chunk, 0:1], stats_in[chunk, 1:2]
        top[...] = jnp.broadcast_to(own_top, (8, ROWS))
        total[...] = jnp.zeros((8, ROWS), F32)
        grad_query[chunk] = jnp.zeros((HEAD_SIZE, ROWS), F32)

        def scores_step(limits):
            def step(tile, count):
                here = at(tile, count)
                s = scores(keys[here], rows_q, tile, count, limits)
                probs[here] = s
                top[...] = jnp.maximum(top[...], fold(s, jnp.max))

            return step

        sweep(low, full_low, scores_step(limits), GROUP)
        sweep(full_low, TILES, scores_step(None), GROUP)
        row_top = jnp.max(top[...], axis=0, keepdims=True)
        rescale = jnp.exp2(own_top - row_top)
        out_t[...] = out_in[chunk] * rescale

        def output_step(tile, count):
            here = at(tile, count)
            p = jnp.exp2(probs[here] - row_top)
            probs[here] = p
            total[...] += fold(p, jnp.sum)
            out_t[...] += dot(values_t[:, here], p.astype(BF16), ((1,), (0,)))

        sweep(low, TILES, output_step, GROUP)
        row_total = jnp.sum(total[...], axis=0, keepdims=True) + own_total * rescale
        inverse = 1.0 / row_total
        attended = out_t[...] * inverse
        delta = jnp.sum(rows_d.astype(F32).T * attended, axis=0, keepdims=True)
        store_rows(context_ref, chunk, attended.T)
        stats_ref[chunk, 0:1] = row_top + jnp.log2(row_total)
        stats_ref[chunk, 1:2] = delta

        def gradient_step(tile, count):
            here = at(tile, count)
            w = probs[here] * inverse
            grad_weights = dot(values[here], rows_d, ((1,), (1,)))
            grad_scores = (w * (grad_weights - delta)).astype(BF16)
            grad_values[here] += dot(w.astype(BF16), rows_d, ((1,), (0,)))
            grad_keys[here] += dot(grad_scores, rows_q, ((1,), (0,)))
            grad_query[chunk] += dot(keys_t[:, here], grad_scores, ((1,), (0,)))

        sweep(low, TILES, gradient_step, GROUP)
        hand_over(chunk).start()
        return 0

    lax.fori_loop(0, 4, chunk_step, 0)

    def store(tile, _):
        grad_ref[at(tile), :HEAD_SIZE] = (grad_keys[at(tile)] * SCALE).astype(BF16)
        grad_ref[at(tile), HEAD_SIZE:] = grad_values[at(tile)].astype(BF16)
        return 0

    lax.fori_loop(first, TILES, store, 0)
    for chunk in range(4):
        hand_over(chunk).wait()


def own_backward(
    scalars, begin_ref, qd_ref, mine_ref, other_ref, stats_in, grad_query_in,
    out_0, out_1, out_2, out_3, grad_ref, keys, values,
    keys_t, grad_keys, grad_values, grad_query_t, grad_query, sem,
):
    first = jnp.maximum(scalars[0], 0) // TILE

    def fetch(chunk):
        return pltpu.make_async_copy(
            grad_query_in.at[chunk], grad_query_t.at[chunk], sem.at[chunk]
        )

    for chunk in range(4):
        fetch(chunk).start()

    def keep(tile, k, v):
        keys[at(tile)] = k
        values[at(tile)] = v
        keys_t[:, at(tile)] = k.T
        grad_keys[at(tile)] = jnp.zeros((TILE, HEAD_SIZE), F32)
        grad_values[at(tile)] = jnp.zeros((TILE, HEAD_SIZE), F32)

    load_halves(scalars, first, mine_ref, other_ref, keep)

    def blank(tile, _):
        grad_ref[at(tile)] = jnp.zeros((TILE, 2 * HEAD_SIZE), BF16)
        return 0

    lax.fori_loop(0, first, blank, 0)

    def chunk_step(chunk, _):
        start, low, high, full_low, full_high = own_range(scalars, chunk)
        rows_q = rows_of(qd_ref, chunk, 0)
        rows_d = rows_of(qd_ref, chunk, 1)
        limits = (begin_ref[chunk], position_in_rows(start))
        log_total, delta = stats_in[chunk, 0:1], stats_in[chunk, 1:2]
        fetch(chunk).wait()

        def gradient_step(limits):
            def step(tile, count):
                here = at(tile, count)
                s = scores(keys[here], rows_q, tile, count, limits)
                w = jnp.exp2(s - log_total)
                grad_weights = dot(values[here], rows_d, ((1,), (1,)))
                grad_scores = (w * (grad_weights - delta)).astype(BF16)
                grad_values[here] += dot(w.astype(BF16), rows_d, ((1,), (0,)))
                grad_keys[here] += dot(grad_scores, rows_q, ((1,), (0,)))
                grad_query_t[chunk] += dot(keys_t[:, here], grad_scores, ((1,), (0,)))

            return step

        sweep(low, full_low, gradient_step(limits), BACK_GROUP)
        sweep(full_low, full_high, gradient_step(None), BACK_GROUP)
        sweep(full_high, high, gradient_step(limits), BACK_GROUP)
        store_rows(grad_query, (chunk - scalars[9]) & 3, (grad_query_t[chunk] * SCALE).T)
        return 0

    lax.fori_loop(0, 4, chunk_step, 0)

    def store(tile, _):
        grad_ref[at(tile), :HEAD_SIZE] = (grad_keys[at(tile)] * SCALE).astype(BF16)
        grad_ref[at(tile), HEAD_SIZE:] = grad_values[at(tile)].astype(BF16)
        return 0

    lax.fori_loop(first, TILES, store, 0)
    for slot, out in enumerate((out_0, out_1, out_2, out_3)):
        out[...] = grad_query[slot]


def call(kernel, name, gflops, megabytes, outs, scratch, *args, hbm_in=(), hbm_out=(), sems=0):
    vmem, hbm = pl.BlockSpec(memory_space=pltpu.VMEM), pl.BlockSpec(memory_space=pltpu.HBM)
    return pl.pallas_call(
        kernel,
        out_shape=tuple(jax.ShapeDtypeStruct(shape, dtype) for shape, dtype in outs),
        in_specs=[pl.BlockSpec(memory_space=pltpu.SMEM)]
        + [hbm if n in hbm_in else vmem for n in range(1, len(args))],
        out_specs=tuple(hbm if n in hbm_out else vmem for n in range(len(outs))),
        scratch_shapes=[pltpu.VMEM(shape, dtype) for shape, dtype in scratch]
        + ([pltpu.SemaphoreType.DMA((sems,))] if sems else []),
        compiler_params=pltpu.CompilerParams(vmem_limit_bytes=megabytes << 20),
        cost_estimate=pl.CostEstimate(
            flops=gflops * 10**9, bytes_accessed=4 << 20, transcendentals=2 * 10**6
        ),
        name=name,
    )(*args)


STATS = ((4, 2, ROWS), F32)
ACROSS = ((4, HEAD_SIZE, ROWS), F32)
RESULT = ((4, CHUNK, ROWS), BF16)
PIECE = ((CHUNK, ROWS), BF16)
GRADS = ((SPAN, 2 * HEAD_SIZE), BF16)
LINES = ((SPAN, HEAD_SIZE), BF16)
TURNED = ((HEAD_SIZE, SPAN), BF16)
SQUARE = ((SPAN, ROWS), F32)
SUMS = ((SPAN, HEAD_SIZE), F32)
FLAT = ((HEAD_SIZE, ROWS), F32)
EIGHT = ((8, ROWS), F32)


def run_own_forward(scalars, begin, qd, mine, other):
    return call(
        own_forward, "own_forward", 2, 12, (STATS, ACROSS), (LINES, TURNED, SQUARE, EIGHT, EIGHT),
        scalars, begin, qd, mine, other,
    )


def run_before_part(scalars, begin, qd, mine, other, stats, out):
    return call(
        before_part, "before_part", 2, 18, (RESULT, GRADS, STATS, ACROSS),
        (LINES, LINES, TURNED, TURNED, SQUARE, SUMS, SUMS, FLAT, ACROSS, EIGHT, EIGHT),
        scalars, begin, qd, mine, other, stats, out, hbm_out=(3,), sems=4,
    )


def run_own_backward(scalars, begin, qd, mine, other, stats, grad_query):
    return call(
        own_backward, "own_backward", 3, 60, (PIECE,) * 4 + (GRADS,),
        (LINES, LINES, TURNED, SUMS, SUMS, ACROSS, RESULT),
        scalars, begin, qd, mine, other, stats, grad_query, hbm_in=(6,), sems=4,
    )


def small(kernel, name, outs, scalar, *args):
    vmem = pl.BlockSpec(memory_space=pltpu.VMEM)
    smem = [pl.BlockSpec(memory_space=pltpu.SMEM)] if scalar is not None else []
    return pl.pallas_call(
        kernel,
        out_shape=tuple(jax.ShapeDtypeStruct(shape, dtype) for shape, dtype in outs),
        in_specs=smem + [vmem] * len(args),
        out_specs=tuple(vmem for _ in outs),
        compiler_params=pltpu.CompilerParams(vmem_limit_bytes=8 << 20),
        cost_estimate=pl.CostEstimate(flops=10**6, bytes_accessed=2 << 20, transcendentals=0),
        name=name,
    )(*([scalar] if scalar is not None else []), *args)


def pack(y, queries, output_gradient, keys, values):
    def kernel(y_ref, q_ref, d_ref, k_ref, v_ref, qd_ref, one_ref, two_ref, sem):
        moves = []
        for index, source in enumerate((k_ref, v_ref)):
            for head, target in ((y_ref[0] & 1, one_ref), (1 - (y_ref[0] & 1), two_ref)):
                moves.append(
                    (
                        source.at[:, pl.ds(pl.multiple_of(head * HEAD_SIZE, HEAD_SIZE), HEAD_SIZE)],
                        target.at[:, pl.ds(index * HEAD_SIZE, HEAD_SIZE)],
                    )
                )
        for index, source in enumerate((q_ref, d_ref)):
            for d in range(4):
                moves.append(
                    (
                        source.at[:, pl.ds(d * ROWS, ROWS)],
                        qd_ref.at[d, pl.ds(index * CHUNK, CHUNK)],
                    )
                )
        copies = [
            pltpu.make_async_copy(source, target, sem.at[n])
            for n, (source, target) in enumerate(moves)
        ]
        for copy in copies:
            copy.start()
        for copy in copies:
            copy.wait()

    hbm, vmem = pl.BlockSpec(memory_space=pltpu.HBM), pl.BlockSpec(memory_space=pltpu.VMEM)
    half = jax.ShapeDtypeStruct((CHUNK, 2 * HEAD_SIZE), BF16)
    return pl.pallas_call(
        kernel,
        out_shape=(jax.ShapeDtypeStruct((4, 2 * CHUNK, ROWS), BF16), half, half),
        in_specs=[pl.BlockSpec(memory_space=pltpu.SMEM)] + [hbm] * 4,
        out_specs=(vmem,) * 3,
        scratch_shapes=[pltpu.SemaphoreType.DMA((12,))],
        compiler_params=pltpu.CompilerParams(vmem_limit_bytes=60 << 20),
        cost_estimate=pl.CostEstimate(flops=10**6, bytes_accessed=2 << 20, transcendentals=0),
        name="pack",
    )(y, queries, output_gradient, keys, values)


def join(y, *pieces):
    def kernel(y_ref, *refs):
        out = refs[-1]
        for step in range(4):
            group = (y_ref[0] - step) & 3
            out[:, pl.ds(pl.multiple_of(group * ROWS, ROWS), ROWS)] = refs[step][...]

    return small(kernel, "join", (((CHUNK, 4 * ROWS), BF16),), y, *pieces)[0]


def last_sum(grad):
    def kernel(grad_ref, keys_ref, values_ref):
        for head in range(2):
            total = sum(grad_ref[i, head].astype(F32) for i in range(4)).astype(BF16)
            here = slice(head * HEAD_SIZE, (head + 1) * HEAD_SIZE)
            keys_ref[:, here] = total[:, :HEAD_SIZE]
            values_ref[:, here] = total[:, HEAD_SIZE:]

    outs = (((CHUNK, 2 * HEAD_SIZE), BF16),) * 2
    return small(kernel, "last_sum", outs, None, grad)


def columns(value, index, count):
    width = value.shape[1] // count
    return value[:, index * width : (index + 1) * width]


def per_device(queries, key_projection, value_projection, output_gradient, doc_lengths):
    z_hi = lax.axis_index("z_hi").astype(jnp.int32)
    y = lax.axis_index("y").astype(jnp.int32)
    block = lax.axis_index(BLOCK_AXES).astype(jnp.int32)
    blocks = lax.axis_size(BLOCK_AXES)
    own_start = block * SPAN
    qd, one, two = pack(y[None], queries, output_gradient, key_projection, value_projection)
    one = lax.ppermute(one, "y", [(0, 0), (1, 2), (2, 1), (3, 3)])
    two = lax.ppermute(two, "y", [(0, 2), (1, 0), (2, 3), (3, 1)])
    mine = jnp.where(y < 2, jnp.stack([one, two]), jnp.stack([two, one]))
    qd, mine = lax.optimization_barrier((qd, mine))
    qd = lax.all_to_all(qd, "y", split_axis=0, concat_axis=0, tiled=True)
    mine = lax.all_gather(mine, "z_hi", axis=1, tiled=True)
    qd, mine = lax.optimization_barrier((qd, mine))
    mine = mine.reshape(SPAN // 2, 2 * HEAD_SIZE)
    to_next = [(i, i + 1) for i in range(blocks - 1)]
    other = lax.ppermute(mine, "y", [(0, 1), (1, 0), (2, 3), (3, 2)])
    kv_own = (mine, other)
    kv_before = (lax.ppermute(mine, BLOCK_AXES, to_next), lax.ppermute(other, BLOCK_AXES, to_next))
    docs = doc_lengths.shape[0]
    order = jnp.arange(docs)
    starts = jnp.sum(jnp.where(order[None, :] < order[:, None], doc_lengths[None, :], 0), axis=1)
    chunk_start = (4 * jnp.arange(4, dtype=jnp.int32) + z_hi) * CHUNK + own_start
    position = (chunk_start[:, None] + jnp.arange(CHUNK, dtype=jnp.int32)[None, :])[..., None]
    begin = jnp.max(jnp.where(starts <= position, starts, 0), axis=2).astype(jnp.int32) - own_start
    scalars = jnp.concatenate([begin[:, 0], begin[:, -1], z_hi[None], y[None]])
    begin = jnp.tile(begin, (1, HEADS)).reshape(4, 1, ROWS)

    stats, out = run_own_forward(scalars, begin, qd, *kv_own)
    kv_before, stats, out = lax.optimization_barrier((kv_before, stats, out))
    context, grad_before, stats, grad_query = run_before_part(
        scalars, begin, qd, *kv_before, stats, out
    )
    returned = lax.ppermute(grad_before, BLOCK_AXES, [(i + 1, i) for i in range(blocks - 1)])
    context = lax.all_to_all(context, "y", split_axis=0, concat_axis=0, tiled=True)
    *grad_query, grad_own = run_own_backward(scalars, begin, qd, *kv_own, stats, grad_query)
    context, returned, grad_own = lax.optimization_barrier((context, returned, grad_own))
    grad_own = (grad_own.astype(F32) + returned.astype(F32)).astype(BF16)
    grad = lax.all_to_all(
        grad_own.reshape(4, 4, CHUNK, 2 * HEAD_SIZE), "y", split_axis=0, concat_axis=0, tiled=True
    )

    grad = grad.astype(F32)
    grad = jnp.stack([grad[0] + grad[1], grad[2] + grad[3]], axis=1).astype(BF16)
    grad, *grad_query = lax.optimization_barrier((grad, *grad_query))
    grad = lax.all_to_all(grad, "z_hi", split_axis=0, concat_axis=0, tiled=True)
    pieces = [grad_query[0]] + [
        lax.ppermute(grad_query[step], "y", [(i, (i + step) % 4) for i in range(4)])
        for step in (1, 2, 3)
    ]
    grad_queries = join(y[None], *pieces)
    keys_gradient, values_gradient = last_sum(grad)
    return (
        jnp.concatenate([context[i] for i in range(4)], axis=1),
        grad_queries,
        keys_gradient,
        values_gradient,
    )


def solution(mesh):
    order = [mesh.axis_names.index(name) for name in ("uly", "blk")]
    devices = np.transpose(mesh.devices, order).reshape(4, 4, 4, 4, 2)
    fine = Mesh(devices, ("y", "z_hi", "z_lo", "x", "core"))
    rows = P(TOKEN_AXES, None)
    return jax.shard_map(
        per_device, mesh=fine, in_specs=(rows, rows, rows, rows, P()),
        out_specs=(rows, rows, rows, rows), check_vma=False,
    )
```

```python
import math

import jax
import jax.numpy as jnp
import numpy as np
from jax import lax
from jax.experimental import pallas as pl
from jax.experimental.pallas import tpu as pltpu
from jax.sharding import Mesh
from jax.sharding import PartitionSpec as P

HEAD_SIZE = 128
SPAN = 2048
CHUNK = 128
TILE = 256
TILES = SPAN // TILE
GROUP = (4, 2, 1)
BACK_GROUP = (2, 1)
HEADS = 4
ROWS = HEADS * CHUNK
BLOCK_AXES = ("z_lo", "x", "core")
TOKEN_AXES = ("z_lo", "x", "core", "y", "z_hi")
SCALE = 1.0 / math.sqrt(HEAD_SIZE)
LOG2_SCALE = SCALE * math.log2(math.e)
F32, BF16 = jnp.float32, jnp.bfloat16


def dot(a, b, contract):
    return lax.dot_general(a, b, (contract, ((), ())), preferred_element_type=F32)


def rows_of(ref, chunk, part):
    block = ref[chunk, part * CHUNK : (part + 1) * CHUNK]
    return jnp.concatenate(
        [block[:, h * HEAD_SIZE : (h + 1) * HEAD_SIZE] for h in range(HEADS)], axis=0
    )


def store_rows(ref, chunk, value):
    for h in range(HEADS):
        ref[chunk, :, h * HEAD_SIZE : (h + 1) * HEAD_SIZE] = value[h * CHUNK : (h + 1) * CHUNK]


def at(tile, count=1):
    return pl.ds(pl.multiple_of(tile * TILE, TILE), count * TILE)


def sweep(low, high, step, sizes):
    for size in sizes:
        groups = (high - low) // size

        def many(i, _, low=low, size=size):
            step(low + i * size, size)
            return 0

        lax.fori_loop(0, groups, many, 0)
        low = low + groups * size


def own_range(scalars, chunk):
    start = (4 * chunk + scalars[8]) * CHUNK
    low = jnp.maximum(scalars[chunk], 0) // TILE
    high = (start + CHUNK - 1) // TILE + 1
    full_low = jnp.minimum((jnp.maximum(scalars[4 + chunk], 0) + TILE - 1) // TILE, high)
    full_high = jnp.clip((start + 1) // TILE, full_low, high)
    return start, low, high, full_low, full_high


def before_range(scalars, chunk):
    low = jnp.minimum(scalars[chunk] + SPAN, SPAN) // TILE
    full_low = jnp.minimum((scalars[4 + chunk] + SPAN + TILE - 1) // TILE, TILES)
    return low, full_low


def position_in_rows(start):
    return start + (lax.broadcasted_iota(jnp.int32, (1, ROWS), 1) & (CHUNK - 1))


def load_halves(scalars, first, mine_ref, other_ref, keep):
    half = TILES // 2
    for ref, which in ((mine_ref, scalars[9] & 1), (other_ref, 1 - (scalars[9] & 1))):
        shift = which * half

        def body(tile, _, ref=ref, shift=shift):
            both = ref[at(tile - shift)]
            keep(tile, both[:, :HEAD_SIZE], both[:, HEAD_SIZE:])
            return 0

        lax.fori_loop(jnp.maximum(first, shift), shift + half, body, 0)


def scores(keys, rows_q, tile, count, limits):
    s = LOG2_SCALE * dot(keys, rows_q, ((1,), (1,)))
    if limits is not None:
        begin, last = limits
        key_pos = tile * TILE + lax.broadcasted_iota(jnp.int32, (count * TILE, ROWS), 0)
        allowed = key_pos >= begin
        if last is not None:
            allowed &= key_pos <= last
        s = jnp.where(allowed, s, -1e30)
    return s


def fold(value, how):
    return how(value.reshape(value.shape[0] // 8, 8, ROWS), axis=0)


def own_forward(
    scalars, begin_ref, qd_ref, mine_ref, other_ref,
    stats_ref, out_ref, keys, values_t, probs, top, total,
):
    first = jnp.maximum(scalars[0], 0) // TILE

    def keep(tile, k, v):
        keys[at(tile)] = k
        values_t[:, at(tile)] = v.T

    load_halves(scalars, first, mine_ref, other_ref, keep)

    def chunk_step(chunk, _):
        start, low, high, full_low, full_high = own_range(scalars, chunk)
        rows_q = rows_of(qd_ref, chunk, 0)
        limits = (begin_ref[chunk], position_in_rows(start))
        top[...] = jnp.full((8, ROWS), -1e30, F32)
        total[...] = jnp.zeros((8, ROWS), F32)
        out_ref[chunk] = jnp.zeros((HEAD_SIZE, ROWS), F32)

        def scores_step(limits):
            def step(tile, count):
                here = at(tile, count)
                s = scores(keys[here], rows_q, tile, count, limits)
                probs[here] = s
                top[...] = jnp.maximum(top[...], fold(s, jnp.max))

            return step

        sweep(low, full_low, scores_step(limits), GROUP)
        sweep(full_low, full_high, scores_step(None), GROUP)
        sweep(full_high, high, scores_step(limits), GROUP)
        row_top = jnp.max(top[...], axis=0, keepdims=True)

        def output_step(tile, count):
            here = at(tile, count)
            p = jnp.exp2(probs[here] - row_top)
            total[...] += fold(p, jnp.sum)
            out_ref[chunk] += dot(values_t[:, here], p.astype(BF16), ((1,), (0,)))

        sweep(low, high, output_step, GROUP)
        stats_ref[chunk, 0:1] = row_top
        stats_ref[chunk, 1:2] = jnp.sum(total[...], axis=0, keepdims=True)
        return 0

    lax.fori_loop(0, 4, chunk_step, 0)


def before_part(
    scalars, begin_ref, qd_ref, mine_ref, other_ref, stats_in, out_in,
    context_ref, grad_ref, handed_ref, keys, values,
    keys_t, values_t, probs, grad_keys, grad_values, out_t, handed, top, total, sem,
):
    first = jnp.minimum(scalars[0] + SPAN, SPAN) // TILE

    def keep(tile, k, v):
        keys[at(tile)] = k
        values[at(tile)] = v
        keys_t[:, at(tile)] = k.T
        values_t[:, at(tile)] = v.T
        grad_keys[at(tile)] = jnp.zeros((TILE, HEAD_SIZE), F32)
        grad_values[at(tile)] = jnp.zeros((TILE, HEAD_SIZE), F32)

    load_halves(scalars, first, mine_ref, other_ref, keep)

    def blank(tile, _):
        grad_ref[at(tile)] = jnp.zeros((TILE, 2 * HEAD_SIZE), BF16)
        return 0

    lax.fori_loop(0, first, blank, 0)

    def hand_over(chunk):
        return pltpu.make_async_copy(
            handed.at[chunk], handed_ref.at[chunk], sem.at[chunk]
        )

    def chunk_step(chunk, _):
        low, full_low = before_range(scalars, chunk)
        rows_q = rows_of(qd_ref, chunk, 0)
        rows_d = rows_of(qd_ref, chunk, 1)
        limits = (begin_ref[chunk] + SPAN, None)
        own_top, own_total = stats_in[chunk, 0:1], stats_in[chunk, 1:2]
        top[...] = jnp.broadcast_to(own_top, (8, ROWS))
        total[...] = jnp.zeros((8, ROWS), F32)
        handed[chunk, :HEAD_SIZE] = jnp.zeros((HEAD_SIZE, ROWS), F32)

        def scores_step(limits):
            def step(tile, count):
                here = at(tile, count)
                s = scores(keys[here], rows_q, tile, count, limits)
                probs[here] = s
                top[...] = jnp.maximum(top[...], fold(s, jnp.max))

            return step

        sweep(low, full_low, scores_step(limits), GROUP)
        sweep(full_low, TILES, scores_step(None), GROUP)
        row_top = jnp.max(top[...], axis=0, keepdims=True)
        rescale = jnp.exp2(own_top - row_top)
        out_t[...] = out_in[chunk] * rescale

        def output_step(tile, count):
            here = at(tile, count)
            p = jnp.exp2(probs[here] - row_top)
            probs[here] = p
            total[...] += fold(p, jnp.sum)
            out_t[...] += dot(values_t[:, here], p.astype(BF16), ((1,), (0,)))

        sweep(low, TILES, output_step, GROUP)
        row_total = jnp.sum(total[...], axis=0, keepdims=True) + own_total * rescale
        inverse = 1.0 / row_total
        attended = out_t[...] * inverse
        delta = jnp.sum(rows_d.T.astype(F32) * attended, axis=0, keepdims=True)
        store_rows(context_ref, chunk, attended.astype(BF16).T)
        handed[chunk, HEAD_SIZE : HEAD_SIZE + 1] = row_top + jnp.log2(row_total)
        handed[chunk, HEAD_SIZE + 1 : HEAD_SIZE + 2] = delta

        def gradient_step(tile, count):
            here = at(tile, count)
            w = probs[here] * inverse
            grad_weights = dot(values[here], rows_d, ((1,), (1,)))
            grad_scores = (w * (grad_weights - delta)).astype(BF16)
            grad_values[here] += dot(w.astype(BF16), rows_d, ((1,), (0,)))
            grad_keys[here] += dot(grad_scores, rows_q, ((1,), (0,)))
            handed[chunk, :HEAD_SIZE] += dot(keys_t[:, here], grad_scores, ((1,), (0,)))

        sweep(low, TILES, gradient_step, GROUP)
        hand_over(chunk).start()
        return 0

    lax.fori_loop(0, 4, chunk_step, 0)

    def store(tile, _):
        grad_ref[at(tile), :HEAD_SIZE] = (grad_keys[at(tile)] * SCALE).astype(BF16)
        grad_ref[at(tile), HEAD_SIZE:] = grad_values[at(tile)].astype(BF16)
        return 0

    lax.fori_loop(first, TILES, store, 0)
    for chunk in range(4):
        hand_over(chunk).wait()


def own_backward(
    scalars, begin_ref, qd_ref, mine_ref, other_ref, handed_in,
    out_0, out_1, out_2, out_3, grad_ref, keys, values,
    keys_t, grad_keys, grad_values, handed, grad_query, sem,
):
    first = jnp.maximum(scalars[0], 0) // TILE

    def fetch(chunk):
        return pltpu.make_async_copy(
            handed_in.at[chunk], handed.at[chunk], sem.at[chunk]
        )

    for chunk in range(4):
        fetch(chunk).start()

    def keep(tile, k, v):
        keys[at(tile)] = k
        values[at(tile)] = v
        keys_t[:, at(tile)] = k.T
        grad_keys[at(tile)] = jnp.zeros((TILE, HEAD_SIZE), F32)
        grad_values[at(tile)] = jnp.zeros((TILE, HEAD_SIZE), F32)

    load_halves(scalars, first, mine_ref, other_ref, keep)

    def blank(tile, _):
        grad_ref[at(tile)] = jnp.zeros((TILE, 2 * HEAD_SIZE), BF16)
        return 0

    lax.fori_loop(0, first, blank, 0)

    def chunk_step(chunk, _):
        start, low, high, full_low, full_high = own_range(scalars, chunk)
        rows_q = rows_of(qd_ref, chunk, 0)
        rows_d = rows_of(qd_ref, chunk, 1)
        limits = (begin_ref[chunk], position_in_rows(start))
        fetch(chunk).wait()
        log_total = handed[chunk, HEAD_SIZE : HEAD_SIZE + 1]
        delta = handed[chunk, HEAD_SIZE + 1 : HEAD_SIZE + 2]

        def gradient_step(limits):
            def step(tile, count):
                here = at(tile, count)
                s = scores(keys[here], rows_q, tile, count, limits)
                w = jnp.exp2(s - log_total)
                grad_weights = dot(values[here], rows_d, ((1,), (1,)))
                grad_scores = (w * (grad_weights - delta)).astype(BF16)
                grad_values[here] += dot(w.astype(BF16), rows_d, ((1,), (0,)))
                grad_keys[here] += dot(grad_scores, rows_q, ((1,), (0,)))
                handed[chunk, :HEAD_SIZE] += dot(keys_t[:, here], grad_scores, ((1,), (0,)))

            return step

        sweep(low, full_low, gradient_step(limits), BACK_GROUP)
        sweep(full_low, full_high, gradient_step(None), BACK_GROUP)
        sweep(full_high, high, gradient_step(limits), BACK_GROUP)
        store_rows(grad_query, (chunk - scalars[9]) & 3, (handed[chunk, :HEAD_SIZE] * SCALE).astype(BF16).T)
        return 0

    lax.fori_loop(0, 4, chunk_step, 0)

    def store(tile, _):
        grad_ref[at(tile), :HEAD_SIZE] = (grad_keys[at(tile)] * SCALE).astype(BF16)
        grad_ref[at(tile), HEAD_SIZE:] = grad_values[at(tile)].astype(BF16)
        return 0

    lax.fori_loop(first, TILES, store, 0)
    for slot, out in enumerate((out_0, out_1, out_2, out_3)):
        out[...] = grad_query[slot]


def call(kernel, name, gflops, megabytes, outs, scratch, *args, hbm_in=(), hbm_out=(), sems=0):
    vmem, hbm = pl.BlockSpec(memory_space=pltpu.VMEM), pl.BlockSpec(memory_space=pltpu.HBM)
    return pl.pallas_call(
        kernel,
        out_shape=tuple(jax.ShapeDtypeStruct(shape, dtype) for shape, dtype in outs),
        in_specs=[pl.BlockSpec(memory_space=pltpu.SMEM)]
        + [hbm if n in hbm_in else vmem for n in range(1, len(args))],
        out_specs=tuple(hbm if n in hbm_out else vmem for n in range(len(outs))),
        scratch_shapes=[pltpu.VMEM(shape, dtype) for shape, dtype in scratch]
        + ([pltpu.SemaphoreType.DMA((sems,))] if sems else []),
        compiler_params=pltpu.CompilerParams(vmem_limit_bytes=megabytes << 20),
        cost_estimate=pl.CostEstimate(
            flops=gflops * 10**9, bytes_accessed=4 << 20, transcendentals=2 * 10**6
        ),
        name=name,
    )(*args)


STATS = ((4, 2, ROWS), F32)
ACROSS = ((4, HEAD_SIZE, ROWS), F32)
HANDED = ((4, HEAD_SIZE + 8, ROWS), F32)
RESULT = ((4, CHUNK, ROWS), BF16)
PIECE = ((CHUNK, ROWS), BF16)
GRADS = ((SPAN, 2 * HEAD_SIZE), BF16)
LINES = ((SPAN, HEAD_SIZE), BF16)
TURNED = ((HEAD_SIZE, SPAN), BF16)
SQUARE = ((SPAN, ROWS), F32)
SUMS = ((SPAN, HEAD_SIZE), F32)
FLAT = ((HEAD_SIZE, ROWS), F32)
EIGHT = ((8, ROWS), F32)


def run_own_forward(scalars, begin, qd, mine, other):
    return call(
        own_forward, "own_forward", 2, 12, (STATS, ACROSS), (LINES, TURNED, SQUARE, EIGHT, EIGHT),
        scalars, begin, qd, mine, other,
    )


def run_before_part(scalars, begin, qd, mine, other, stats, out):
    return call(
        before_part, "before_part", 2, 18, (RESULT, GRADS, HANDED),
        (LINES, LINES, TURNED, TURNED, SQUARE, SUMS, SUMS, FLAT, HANDED, EIGHT, EIGHT),
        scalars, begin, qd, mine, other, stats, out, hbm_out=(2,), sems=4,
    )


def run_own_backward(scalars, begin, qd, mine, other, handed):
    return call(
        own_backward, "own_backward", 3, 60, (PIECE,) * 4 + (GRADS,),
        (LINES, LINES, TURNED, SUMS, SUMS, HANDED, RESULT),
        scalars, begin, qd, mine, other, handed, hbm_in=(5,), sems=4,
    )


def small(kernel, name, outs, scalar, *args):
    vmem = pl.BlockSpec(memory_space=pltpu.VMEM)
    smem = [pl.BlockSpec(memory_space=pltpu.SMEM)] if scalar is not None else []
    return pl.pallas_call(
        kernel,
        out_shape=tuple(jax.ShapeDtypeStruct(shape, dtype) for shape, dtype in outs),
        in_specs=smem + [vmem] * len(args),
        out_specs=tuple(vmem for _ in outs),
        compiler_params=pltpu.CompilerParams(vmem_limit_bytes=8 << 20),
        cost_estimate=pl.CostEstimate(flops=10**6, bytes_accessed=2 << 20, transcendentals=0),
        name=name,
    )(*([scalar] if scalar is not None else []), *args)


def copy_all(moves, sem):
    copies = [
        pltpu.make_async_copy(source, target, sem.at[n]) for n, (source, target) in enumerate(moves)
    ]
    for copy in copies:
        copy.start()
    for copy in copies:
        copy.wait()


def packing(kernel, name, outs, scalar, *args, sems):
    hbm, vmem = pl.BlockSpec(memory_space=pltpu.HBM), pl.BlockSpec(memory_space=pltpu.VMEM)
    smem = [pl.BlockSpec(memory_space=pltpu.SMEM)] if scalar is not None else []
    return pl.pallas_call(
        kernel,
        out_shape=tuple(jax.ShapeDtypeStruct(shape, dtype) for shape, dtype in outs),
        in_specs=smem + [hbm] * len(args),
        out_specs=(vmem,) * len(outs),
        scratch_shapes=[pltpu.SemaphoreType.DMA((sems,))],
        compiler_params=pltpu.CompilerParams(vmem_limit_bytes=60 << 20),
        cost_estimate=pl.CostEstimate(flops=10**6, bytes_accessed=2 << 20, transcendentals=0),
        name=name,
    )(*([scalar] if scalar is not None else []), *args)


def pack_rows(queries, output_gradient):
    def kernel(q_ref, d_ref, qd_ref, sem):
        copy_all(
            [
                (
                    source.at[:, pl.ds(d * ROWS, ROWS)],
                    qd_ref.at[d, pl.ds(index * CHUNK, CHUNK)],
                )
                for index, source in enumerate((q_ref, d_ref))
                for d in range(4)
            ],
            sem,
        )

    outs = (((4, 2 * CHUNK, ROWS), BF16),)
    return packing(kernel, "pack_rows", outs, None, queries, output_gradient, sems=8)[0]


def pack_heads(y, keys, values):
    def kernel(y_ref, k_ref, v_ref, one_ref, two_ref, sem):
        parity = y_ref[0] & 1
        copy_all(
            [
                (
                    source.at[:, pl.ds(pl.multiple_of(head * HEAD_SIZE, HEAD_SIZE), HEAD_SIZE)],
                    target.at[:, pl.ds(index * HEAD_SIZE, HEAD_SIZE)],
                )
                for index, source in enumerate((k_ref, v_ref))
                for head, target in ((parity, one_ref), (1 - parity, two_ref))
            ],
            sem,
        )

    outs = (((CHUNK, 2 * HEAD_SIZE), BF16),) * 2
    return packing(kernel, "pack_heads", outs, y, keys, values, sems=4)


def pair_sum(grad):
    def kernel(grad_ref, out_ref):
        for place in range(4):
            for head in range(2):
                out_ref[place, head] = (
                    grad_ref[2 * head, place].astype(F32) + grad_ref[2 * head + 1, place].astype(F32)
                ).astype(BF16)

    return small(kernel, "pair_sum", (((4, 2, CHUNK, 2 * HEAD_SIZE), BF16),), None, grad)[0]


def join(y, *pieces):
    def kernel(y_ref, *refs):
        out = refs[-1]
        for step in range(4):
            group = (y_ref[0] - step) & 3
            out[:, pl.ds(pl.multiple_of(group * ROWS, ROWS), ROWS)] = refs[step][...]

    return small(kernel, "join", (((CHUNK, 4 * ROWS), BF16),), y, *pieces)[0]


def last_sum(grad):
    def kernel(grad_ref, keys_ref, values_ref):
        for head in range(2):
            total = sum(grad_ref[i, head].astype(F32) for i in range(4)).astype(BF16)
            here = slice(head * HEAD_SIZE, (head + 1) * HEAD_SIZE)
            keys_ref[:, here] = total[:, :HEAD_SIZE]
            values_ref[:, here] = total[:, HEAD_SIZE:]

    outs = (((CHUNK, 2 * HEAD_SIZE), BF16),) * 2
    return small(kernel, "last_sum", outs, None, grad)


def columns(value, index, count):
    width = value.shape[1] // count
    return value[:, index * width : (index + 1) * width]


def per_device(queries, key_projection, value_projection, output_gradient, doc_lengths):
    z_hi = lax.axis_index("z_hi").astype(jnp.int32)
    y = lax.axis_index("y").astype(jnp.int32)
    block = lax.axis_index(BLOCK_AXES).astype(jnp.int32)
    blocks = lax.axis_size(BLOCK_AXES)
    own_start = block * SPAN
    one, two = pack_heads(y[None], key_projection, value_projection)
    qd = pack_rows(queries, output_gradient)
    one = lax.ppermute(one, "y", [(0, 0), (1, 2), (2, 1), (3, 3)])
    two = lax.ppermute(two, "y", [(0, 2), (1, 0), (2, 3), (3, 1)])
    mine = jnp.where(y < 2, jnp.stack([one, two]), jnp.stack([two, one]))
    qd, mine = lax.optimization_barrier((qd, mine))
    qd = lax.all_to_all(qd, "y", split_axis=0, concat_axis=0, tiled=True)
    mine = lax.all_gather(mine, "z_hi", axis=1, tiled=True)
    qd, mine = lax.optimization_barrier((qd, mine))
    mine = mine.reshape(SPAN // 2, 2 * HEAD_SIZE)
    to_next = [(i, i + 1) for i in range(blocks - 1)]
    other = lax.ppermute(mine, "y", [(0, 1), (1, 0), (2, 3), (3, 2)])
    kv_own = (mine, other)
    kv_before = (lax.ppermute(mine, BLOCK_AXES, to_next), lax.ppermute(other, BLOCK_AXES, to_next))
    docs = doc_lengths.shape[0]
    order = jnp.arange(docs)
    starts = jnp.sum(jnp.where(order[None, :] < order[:, None], doc_lengths[None, :], 0), axis=1)
    chunk_start = (4 * jnp.arange(4, dtype=jnp.int32) + z_hi) * CHUNK + own_start
    position = (chunk_start[:, None] + jnp.arange(CHUNK, dtype=jnp.int32)[None, :])[..., None]
    begin = jnp.max(jnp.where(starts <= position, starts, 0), axis=2).astype(jnp.int32) - own_start
    scalars = jnp.concatenate([begin[:, 0], begin[:, -1], z_hi[None], y[None]])
    begin = jnp.tile(begin, (1, HEADS)).reshape(4, 1, ROWS)

    stats, out = run_own_forward(scalars, begin, qd, *kv_own)
    kv_before, stats, out = lax.optimization_barrier((kv_before, stats, out))
    context, grad_before, handed = run_before_part(
        scalars, begin, qd, *kv_before, stats, out
    )
    returned = lax.ppermute(grad_before, BLOCK_AXES, [(i + 1, i) for i in range(blocks - 1)])
    context = lax.all_to_all(context, "y", split_axis=0, concat_axis=0, tiled=True)
    *grad_query, grad_own = run_own_backward(scalars, begin, qd, *kv_own, handed)
    context, returned, grad_own = lax.optimization_barrier((context, returned, grad_own))
    grad_own = (grad_own.astype(F32) + returned.astype(F32)).astype(BF16)
    grad = lax.all_to_all(
        grad_own.reshape(4, 4, CHUNK, 2 * HEAD_SIZE), "y", split_axis=0, concat_axis=0, tiled=True
    )

    grad = pair_sum(grad)
    grad, *grad_query = lax.optimization_barrier((grad, *grad_query))
    grad = lax.all_to_all(grad, "z_hi", split_axis=0, concat_axis=0, tiled=True)
    pieces = [grad_query[0]] + [
        lax.ppermute(grad_query[step], "y", [(i, (i + step) % 4) for i in range(4)])
        for step in (1, 2, 3)
    ]
    grad_queries = join(y[None], *pieces)
    keys_gradient, values_gradient = last_sum(grad)
    return (
        jnp.concatenate([context[i] for i in range(4)], axis=1),
        grad_queries,
        keys_gradient,
        values_gradient,
    )


def solution(mesh):
    order = [mesh.axis_names.index(name) for name in ("uly", "blk")]
    devices = np.transpose(mesh.devices, order).reshape(4, 4, 4, 4, 2)
    fine = Mesh(devices, ("y", "z_hi", "z_lo", "x", "core"))
    rows = P(TOKEN_AXES, None)
    return jax.shard_map(
        per_device, mesh=fine, in_specs=(rows, rows, rows, rows, P()),
        out_specs=(rows, rows, rows, rows), check_vma=False,
    )
```

```python
import math

import jax
import jax.numpy as jnp
import numpy as np
from jax import lax
from jax.experimental import pallas as pl
from jax.experimental.pallas import tpu as pltpu
from jax.sharding import Mesh
from jax.sharding import PartitionSpec as P

HEAD_SIZE = 128
SPAN = 2048
CHUNK = 128
TILE = 256
TILES = SPAN // TILE
GROUP = (4, 2, 1)
BACK_GROUP = (2, 1)
HEADS = 4
ROWS = HEADS * CHUNK
BLOCK_AXES = ("z_lo", "x", "core")
TOKEN_AXES = ("z_lo", "x", "core", "y", "z_hi")
SCALE = 1.0 / math.sqrt(HEAD_SIZE)
LOG2_SCALE = SCALE * math.log2(math.e)
F32, BF16 = jnp.float32, jnp.bfloat16


def dot(a, b, contract):
    return lax.dot_general(a, b, (contract, ((), ())), preferred_element_type=F32)


def rows_of(ref, chunk, part):
    block = ref[chunk, part * CHUNK : (part + 1) * CHUNK]
    return jnp.concatenate(
        [block[:, h * HEAD_SIZE : (h + 1) * HEAD_SIZE] for h in range(HEADS)], axis=0
    )


def store_rows(ref, chunk, value):
    for h in range(HEADS):
        ref[chunk, :, h * HEAD_SIZE : (h + 1) * HEAD_SIZE] = value[h * CHUNK : (h + 1) * CHUNK]


def at(tile, count=1):
    return pl.ds(pl.multiple_of(tile * TILE, TILE), count * TILE)


def sweep(low, high, step, sizes):
    for size in sizes:
        groups = (high - low) // size

        def many(i, _, low=low, size=size):
            step(low + i * size, size)
            return 0

        lax.fori_loop(0, groups, many, 0)
        low = low + groups * size


def own_range(scalars, chunk):
    start = (4 * chunk + scalars[8]) * CHUNK
    low = jnp.maximum(scalars[chunk], 0) // TILE
    high = (start + CHUNK - 1) // TILE + 1
    full_low = jnp.minimum((jnp.maximum(scalars[4 + chunk], 0) + TILE - 1) // TILE, high)
    full_high = jnp.clip((start + 1) // TILE, full_low, high)
    return start, low, high, full_low, full_high


def before_range(scalars, chunk):
    low = jnp.minimum(scalars[chunk] + SPAN, SPAN) // TILE
    full_low = jnp.minimum((scalars[4 + chunk] + SPAN + TILE - 1) // TILE, TILES)
    return low, full_low


def position_in_rows(start):
    return start + (lax.broadcasted_iota(jnp.int32, (1, ROWS), 1) & (CHUNK - 1))


def load_quads(scalars, first, quads, keep):
    span = TILES // 4
    for place, ref in enumerate(quads):
        shift = (scalars[9] ^ place) * span

        def body(tile, _, ref=ref, shift=shift):
            both = ref[at(tile - shift)]
            keep(tile, both[:, :HEAD_SIZE], both[:, HEAD_SIZE:])
            return 0

        lax.fori_loop(jnp.maximum(first, shift), shift + span, body, 0)


def scores(keys, rows_q, tile, count, limits):
    s = LOG2_SCALE * dot(keys, rows_q, ((1,), (1,)))
    if limits is not None:
        begin, last = limits
        key_pos = tile * TILE + lax.broadcasted_iota(jnp.int32, (count * TILE, ROWS), 0)
        allowed = key_pos >= begin
        if last is not None:
            allowed &= key_pos <= last
        s = jnp.where(allowed, s, -1e30)
    return s


def fold(value, how):
    return how(value.reshape(value.shape[0] // 8, 8, ROWS), axis=0)


def own_forward(
    scalars, begin_ref, qd_ref, quad_0, quad_1, quad_2, quad_3,
    stats_ref, out_ref, keys, values_t, probs, top, total,
):
    first = jnp.maximum(scalars[0], 0) // TILE

    def keep(tile, k, v):
        keys[at(tile)] = k
        values_t[:, at(tile)] = v.T

    load_quads(scalars, first, (quad_0, quad_1, quad_2, quad_3), keep)

    def chunk_step(chunk, _):
        start, low, high, full_low, full_high = own_range(scalars, chunk)
        rows_q = rows_of(qd_ref, chunk, 0)
        limits = (begin_ref[chunk], position_in_rows(start))
        top[...] = jnp.full((8, ROWS), -1e30, F32)
        total[...] = jnp.zeros((8, ROWS), F32)
        out_ref[chunk] = jnp.zeros((HEAD_SIZE, ROWS), F32)

        def scores_step(limits):
            def step(tile, count):
                here = at(tile, count)
                s = scores(keys[here], rows_q, tile, count, limits)
                probs[here] = s
                top[...] = jnp.maximum(top[...], fold(s, jnp.max))

            return step

        sweep(low, full_low, scores_step(limits), GROUP)
        sweep(full_low, full_high, scores_step(None), GROUP)
        sweep(full_high, high, scores_step(limits), GROUP)
        row_top = jnp.max(top[...], axis=0, keepdims=True)

        def output_step(tile, count):
            here = at(tile, count)
            p = jnp.exp2(probs[here] - row_top)
            total[...] += fold(p, jnp.sum)
            out_ref[chunk] += dot(values_t[:, here], p.astype(BF16), ((1,), (0,)))

        sweep(low, high, output_step, GROUP)
        stats_ref[chunk, 0:1] = row_top
        stats_ref[chunk, 1:2] = jnp.sum(total[...], axis=0, keepdims=True)
        return 0

    lax.fori_loop(0, 4, chunk_step, 0)


def before_part(
    scalars, begin_ref, qd_ref, quad_0, quad_1, quad_2, quad_3, stats_in, out_in,
    context_ref, grad_ref, handed_ref, keys, values,
    keys_t, values_t, probs, grad_keys, grad_values, out_t, handed, top, total, sem,
):
    first = jnp.minimum(scalars[0] + SPAN, SPAN) // TILE

    def keep(tile, k, v):
        keys[at(tile)] = k
        values[at(tile)] = v
        keys_t[:, at(tile)] = k.T
        values_t[:, at(tile)] = v.T
        grad_keys[at(tile)] = jnp.zeros((TILE, HEAD_SIZE), F32)
        grad_values[at(tile)] = jnp.zeros((TILE, HEAD_SIZE), F32)

    load_quads(scalars, first, (quad_0, quad_1, quad_2, quad_3), keep)

    def blank(tile, _):
        grad_ref[at(tile)] = jnp.zeros((TILE, 2 * HEAD_SIZE), BF16)
        return 0

    lax.fori_loop(0, first, blank, 0)

    def hand_over(chunk):
        return pltpu.make_async_copy(
            handed.at[chunk], handed_ref.at[chunk], sem.at[chunk]
        )

    def chunk_step(chunk, _):
        low, full_low = before_range(scalars, chunk)
        rows_q = rows_of(qd_ref, chunk, 0)
        rows_d = rows_of(qd_ref, chunk, 1)
        limits = (begin_ref[chunk] + SPAN, None)
        own_top, own_total = stats_in[chunk, 0:1], stats_in[chunk, 1:2]
        top[...] = jnp.broadcast_to(own_top, (8, ROWS))
        total[...] = jnp.zeros((8, ROWS), F32)
        handed[chunk, :HEAD_SIZE] = jnp.zeros((HEAD_SIZE, ROWS), F32)

        def scores_step(limits):
            def step(tile, count):
                here = at(tile, count)
                s = scores(keys[here], rows_q, tile, count, limits)
                probs[here] = s
                top[...] = jnp.maximum(top[...], fold(s, jnp.max))

            return step

        sweep(low, full_low, scores_step(limits), GROUP)
        sweep(full_low, TILES, scores_step(None), GROUP)
        row_top = jnp.max(top[...], axis=0, keepdims=True)
        rescale = jnp.exp2(own_top - row_top)
        out_t[...] = out_in[chunk] * rescale

        def output_step(tile, count):
            here = at(tile, count)
            p = jnp.exp2(probs[here] - row_top)
            probs[here] = p
            total[...] += fold(p, jnp.sum)
            out_t[...] += dot(values_t[:, here], p.astype(BF16), ((1,), (0,)))

        sweep(low, TILES, output_step, GROUP)
        row_total = jnp.sum(total[...], axis=0, keepdims=True) + own_total * rescale
        inverse = 1.0 / row_total
        attended = out_t[...] * inverse
        delta = jnp.sum(rows_d.T.astype(F32) * attended, axis=0, keepdims=True)
        store_rows(context_ref, chunk, attended.astype(BF16).T)
        handed[chunk, HEAD_SIZE : HEAD_SIZE + 1] = row_top + jnp.log2(row_total)
        handed[chunk, HEAD_SIZE + 1 : HEAD_SIZE + 2] = delta

        def gradient_step(tile, count):
            here = at(tile, count)
            w = probs[here] * inverse
            grad_weights = dot(values[here], rows_d, ((1,), (1,)))
            grad_scores = (w * (grad_weights - delta)).astype(BF16)
            grad_values[here] += dot(w.astype(BF16), rows_d, ((1,), (0,)))
            grad_keys[here] += dot(grad_scores, rows_q, ((1,), (0,)))
            handed[chunk, :HEAD_SIZE] += dot(keys_t[:, here], grad_scores, ((1,), (0,)))

        sweep(low, TILES, gradient_step, GROUP)
        hand_over(chunk).start()
        return 0

    lax.fori_loop(0, 4, chunk_step, 0)

    def store(tile, _):
        grad_ref[at(tile), :HEAD_SIZE] = (grad_keys[at(tile)] * SCALE).astype(BF16)
        grad_ref[at(tile), HEAD_SIZE:] = grad_values[at(tile)].astype(BF16)
        return 0

    lax.fori_loop(first, TILES, store, 0)
    for chunk in range(4):
        hand_over(chunk).wait()


def own_backward(
    scalars, begin_ref, qd_ref, quad_0, quad_1, quad_2, quad_3, handed_in,
    out_0, out_1, out_2, out_3, grad_ref, keys, values,
    keys_t, grad_keys, grad_values, handed, grad_query, sem,
):
    first = jnp.maximum(scalars[0], 0) // TILE

    def fetch(chunk):
        return pltpu.make_async_copy(
            handed_in.at[chunk], handed.at[chunk], sem.at[chunk]
        )

    for chunk in range(4):
        fetch(chunk).start()

    def keep(tile, k, v):
        keys[at(tile)] = k
        values[at(tile)] = v
        keys_t[:, at(tile)] = k.T
        grad_keys[at(tile)] = jnp.zeros((TILE, HEAD_SIZE), F32)
        grad_values[at(tile)] = jnp.zeros((TILE, HEAD_SIZE), F32)

    load_quads(scalars, first, (quad_0, quad_1, quad_2, quad_3), keep)

    def blank(tile, _):
        grad_ref[at(tile)] = jnp.zeros((TILE, 2 * HEAD_SIZE), BF16)
        return 0

    lax.fori_loop(0, first, blank, 0)

    def chunk_step(chunk, _):
        start, low, high, full_low, full_high = own_range(scalars, chunk)
        rows_q = rows_of(qd_ref, chunk, 0)
        rows_d = rows_of(qd_ref, chunk, 1)
        limits = (begin_ref[chunk], position_in_rows(start))
        fetch(chunk).wait()
        log_total = handed[chunk, HEAD_SIZE : HEAD_SIZE + 1]
        delta = handed[chunk, HEAD_SIZE + 1 : HEAD_SIZE + 2]

        def gradient_step(limits):
            def step(tile, count):
                here = at(tile, count)
                s = scores(keys[here], rows_q, tile, count, limits)
                w = jnp.exp2(s - log_total)
                grad_weights = dot(values[here], rows_d, ((1,), (1,)))
                grad_scores = (w * (grad_weights - delta)).astype(BF16)
                grad_values[here] += dot(w.astype(BF16), rows_d, ((1,), (0,)))
                grad_keys[here] += dot(grad_scores, rows_q, ((1,), (0,)))
                handed[chunk, :HEAD_SIZE] += dot(keys_t[:, here], grad_scores, ((1,), (0,)))

            return step

        sweep(low, full_low, gradient_step(limits), BACK_GROUP)
        sweep(full_low, full_high, gradient_step(None), BACK_GROUP)
        sweep(full_high, high, gradient_step(limits), BACK_GROUP)
        store_rows(grad_query, (chunk - scalars[9]) & 3, (handed[chunk, :HEAD_SIZE] * SCALE).astype(BF16).T)
        return 0

    lax.fori_loop(0, 4, chunk_step, 0)

    def store(tile, _):
        grad_ref[at(tile), :HEAD_SIZE] = (grad_keys[at(tile)] * SCALE).astype(BF16)
        grad_ref[at(tile), HEAD_SIZE:] = grad_values[at(tile)].astype(BF16)
        return 0

    lax.fori_loop(first, TILES, store, 0)
    for slot, out in enumerate((out_0, out_1, out_2, out_3)):
        out[...] = grad_query[slot]


def call(kernel, name, gflops, megabytes, outs, scratch, *args, hbm_in=(), hbm_out=(), sems=0):
    vmem, hbm = pl.BlockSpec(memory_space=pltpu.VMEM), pl.BlockSpec(memory_space=pltpu.HBM)
    return pl.pallas_call(
        kernel,
        out_shape=tuple(jax.ShapeDtypeStruct(shape, dtype) for shape, dtype in outs),
        in_specs=[pl.BlockSpec(memory_space=pltpu.SMEM)]
        + [hbm if n in hbm_in else vmem for n in range(1, len(args))],
        out_specs=tuple(hbm if n in hbm_out else vmem for n in range(len(outs))),
        scratch_shapes=[pltpu.VMEM(shape, dtype) for shape, dtype in scratch]
        + ([pltpu.SemaphoreType.DMA((sems,))] if sems else []),
        compiler_params=pltpu.CompilerParams(vmem_limit_bytes=megabytes << 20),
        cost_estimate=pl.CostEstimate(
            flops=gflops * 10**9, bytes_accessed=4 << 20, transcendentals=2 * 10**6
        ),
        name=name,
    )(*args)


STATS = ((4, 2, ROWS), F32)
ACROSS = ((4, HEAD_SIZE, ROWS), F32)
HANDED = ((4, HEAD_SIZE + 8, ROWS), F32)
RESULT = ((4, CHUNK, ROWS), BF16)
PIECE = ((CHUNK, ROWS), BF16)
GRADS = ((SPAN, 2 * HEAD_SIZE), BF16)
LINES = ((SPAN, HEAD_SIZE), BF16)
TURNED = ((HEAD_SIZE, SPAN), BF16)
SQUARE = ((SPAN, ROWS), F32)
SUMS = ((SPAN, HEAD_SIZE), F32)
FLAT = ((HEAD_SIZE, ROWS), F32)
EIGHT = ((8, ROWS), F32)


def run_own_forward(scalars, begin, qd, kv):
    return call(
        own_forward, "own_forward", 2, 12, (STATS, ACROSS), (LINES, TURNED, SQUARE, EIGHT, EIGHT),
        scalars, begin, qd, *kv,
    )


def run_before_part(scalars, begin, qd, kv, stats, out):
    return call(
        before_part, "before_part", 2, 18, (RESULT, GRADS, HANDED),
        (LINES, LINES, TURNED, TURNED, SQUARE, SUMS, SUMS, FLAT, HANDED, EIGHT, EIGHT),
        scalars, begin, qd, *kv, stats, out, hbm_out=(2,), sems=4,
    )


def run_own_backward(scalars, begin, qd, kv, handed):
    return call(
        own_backward, "own_backward", 3, 60, (PIECE,) * 4 + (GRADS,),
        (LINES, LINES, TURNED, SUMS, SUMS, HANDED, RESULT),
        scalars, begin, qd, *kv, handed, hbm_in=(7,), sems=4,
    )


def small(kernel, name, outs, scalar, *args):
    vmem = pl.BlockSpec(memory_space=pltpu.VMEM)
    smem = [pl.BlockSpec(memory_space=pltpu.SMEM)] if scalar is not None else []
    return pl.pallas_call(
        kernel,
        out_shape=tuple(jax.ShapeDtypeStruct(shape, dtype) for shape, dtype in outs),
        in_specs=smem + [vmem] * len(args),
        out_specs=tuple(vmem for _ in outs),
        compiler_params=pltpu.CompilerParams(vmem_limit_bytes=8 << 20),
        cost_estimate=pl.CostEstimate(flops=10**6, bytes_accessed=2 << 20, transcendentals=0),
        name=name,
    )(*([scalar] if scalar is not None else []), *args)


def copy_all(moves, sem):
    copies = [
        pltpu.make_async_copy(source, target, sem.at[n]) for n, (source, target) in enumerate(moves)
    ]
    for copy in copies:
        copy.start()
    for copy in copies:
        copy.wait()


def packing(kernel, name, outs, scalar, *args, sems):
    hbm, vmem = pl.BlockSpec(memory_space=pltpu.HBM), pl.BlockSpec(memory_space=pltpu.VMEM)
    smem = [pl.BlockSpec(memory_space=pltpu.SMEM)] if scalar is not None else []
    return pl.pallas_call(
        kernel,
        out_shape=tuple(jax.ShapeDtypeStruct(shape, dtype) for shape, dtype in outs),
        in_specs=smem + [hbm] * len(args),
        out_specs=(vmem,) * len(outs),
        scratch_shapes=[pltpu.SemaphoreType.DMA((sems,))],
        compiler_params=pltpu.CompilerParams(vmem_limit_bytes=60 << 20),
        cost_estimate=pl.CostEstimate(flops=10**6, bytes_accessed=2 << 20, transcendentals=0),
        name=name,
    )(*([scalar] if scalar is not None else []), *args)


def pack_rows(queries, output_gradient):
    def kernel(q_ref, d_ref, qd_ref, sem):
        copy_all(
            [
                (
                    source.at[:, pl.ds(d * ROWS, ROWS)],
                    qd_ref.at[d, pl.ds(index * CHUNK, CHUNK)],
                )
                for index, source in enumerate((q_ref, d_ref))
                for d in range(4)
            ],
            sem,
        )

    outs = (((4, 2 * CHUNK, ROWS), BF16),)
    return packing(kernel, "pack_rows", outs, None, queries, output_gradient, sems=8)[0]


def pack_heads(y, keys, values):
    def kernel(y_ref, k_ref, v_ref, out_ref, sem):
        mine = y_ref[0] >> 1
        copy_all(
            [
                (
                    source.at[:, pl.ds(pl.multiple_of(head * HEAD_SIZE, HEAD_SIZE), HEAD_SIZE)],
                    out_ref.at[slot, :, pl.ds(index * HEAD_SIZE, HEAD_SIZE)],
                )
                for index, source in enumerate((k_ref, v_ref))
                for slot, head in enumerate((mine, 1 - mine))
            ],
            sem,
        )

    outs = (((2, CHUNK, 2 * HEAD_SIZE), BF16),)
    return packing(kernel, "pack_heads", outs, y, keys, values, sems=4)[0]


def pair_sum(grad):
    def kernel(grad_ref, out_ref):
        for place in range(4):
            for head in range(2):
                out_ref[place, head] = (
                    grad_ref[2 * head, place].astype(F32) + grad_ref[2 * head + 1, place].astype(F32)
                ).astype(BF16)

    return small(kernel, "pair_sum", (((4, 2, CHUNK, 2 * HEAD_SIZE), BF16),), None, grad)[0]


def join(y, *pieces):
    def kernel(y_ref, *refs):
        out = refs[-1]
        for step in range(4):
            group = (y_ref[0] - step) & 3
            out[:, pl.ds(pl.multiple_of(group * ROWS, ROWS), ROWS)] = refs[step][...]

    return small(kernel, "join", (((CHUNK, 4 * ROWS), BF16),), y, *pieces)[0]


def last_sum(grad):
    def kernel(grad_ref, keys_ref, values_ref):
        for head in range(2):
            total = sum(grad_ref[i, head].astype(F32) for i in range(4)).astype(BF16)
            here = slice(head * HEAD_SIZE, (head + 1) * HEAD_SIZE)
            keys_ref[:, here] = total[:, :HEAD_SIZE]
            values_ref[:, here] = total[:, HEAD_SIZE:]

    outs = (((CHUNK, 2 * HEAD_SIZE), BF16),) * 2
    return small(kernel, "last_sum", outs, None, grad)


def columns(value, index, count):
    width = value.shape[1] // count
    return value[:, index * width : (index + 1) * width]


def per_device(queries, key_projection, value_projection, output_gradient, doc_lengths):
    z_hi = lax.axis_index("z_hi").astype(jnp.int32)
    y = lax.axis_index("y").astype(jnp.int32)
    block = lax.axis_index(BLOCK_AXES).astype(jnp.int32)
    blocks = lax.axis_size(BLOCK_AXES)
    own_start = block * SPAN
    kv = pack_heads(y[None], key_projection, value_projection)
    qd = pack_rows(queries, output_gradient)
    qd = lax.all_to_all(qd, "y", split_axis=0, concat_axis=0, tiled=True)
    kv = lax.all_gather(kv, "z_hi", axis=1, tiled=True)
    qd, kv = lax.optimization_barrier((qd, kv))
    across = [(i, i ^ 3) for i in range(4)]
    beside = [(i, i ^ 1) for i in range(4)]
    to_next = [(i, i + 1) for i in range(blocks - 1)]
    quad_0 = kv[0]
    quad_3 = lax.ppermute(kv[1], "y", across)
    quad_1 = lax.ppermute(quad_0, "y", beside)
    quad_2 = lax.ppermute(quad_3, "y", beside)
    kv_own = (quad_0, quad_1, quad_2, quad_3)
    kv_before = tuple(lax.ppermute(quad, BLOCK_AXES, to_next) for quad in kv_own)
    docs = doc_lengths.shape[0]
    order = jnp.arange(docs)
    starts = jnp.sum(jnp.where(order[None, :] < order[:, None], doc_lengths[None, :], 0), axis=1)
    chunk_start = (4 * jnp.arange(4, dtype=jnp.int32) + z_hi) * CHUNK + own_start
    position = (chunk_start[:, None] + jnp.arange(CHUNK, dtype=jnp.int32)[None, :])[..., None]
    begin = jnp.max(jnp.where(starts <= position, starts, 0), axis=2).astype(jnp.int32) - own_start
    scalars = jnp.concatenate([begin[:, 0], begin[:, -1], z_hi[None], y[None]])
    begin = jnp.tile(begin, (1, HEADS)).reshape(4, 1, ROWS)

    stats, out = run_own_forward(scalars, begin, qd, kv_own)
    kv_before, stats, out = lax.optimization_barrier((kv_before, stats, out))
    context, grad_before, handed = run_before_part(
        scalars, begin, qd, kv_before, stats, out
    )
    returned = lax.ppermute(grad_before, BLOCK_AXES, [(i + 1, i) for i in range(blocks - 1)])
    context = lax.all_to_all(context, "y", split_axis=0, concat_axis=0, tiled=True)
    *grad_query, grad_own = run_own_backward(scalars, begin, qd, kv_own, handed)
    context, returned, grad_own = lax.optimization_barrier((context, returned, grad_own))
    grad_own = (grad_own.astype(F32) + returned.astype(F32)).astype(BF16)
    grad = lax.all_to_all(
        grad_own.reshape(4, 4, CHUNK, 2 * HEAD_SIZE), "y", split_axis=0, concat_axis=0, tiled=True
    )

    grad = pair_sum(grad)
    grad, *grad_query = lax.optimization_barrier((grad, *grad_query))
    grad = lax.all_to_all(grad, "z_hi", split_axis=0, concat_axis=0, tiled=True)
    pieces = [grad_query[0]] + [
        lax.ppermute(grad_query[step], "y", [(i, (i + step) % 4) for i in range(4)])
        for step in (1, 2, 3)
    ]
    grad_queries = join(y[None], *pieces)
    keys_gradient, values_gradient = last_sum(grad)
    return (
        jnp.concatenate([context[i] for i in range(4)], axis=1),
        grad_queries,
        keys_gradient,
        values_gradient,
    )


def solution(mesh):
    order = [mesh.axis_names.index(name) for name in ("uly", "blk")]
    devices = np.transpose(mesh.devices, order).reshape(4, 4, 4, 4, 2)
    fine = Mesh(devices, ("y", "z_hi", "z_lo", "x", "core"))
    rows = P(TOKEN_AXES, None)
    return jax.shard_map(
        per_device, mesh=fine, in_specs=(rows, rows, rows, rows, P()),
        out_specs=(rows, rows, rows, rows), check_vma=False,
    )
```

```python
import math

import jax
import jax.numpy as jnp
import numpy as np
from jax import lax
from jax.experimental import pallas as pl
from jax.experimental.pallas import tpu as pltpu
from jax.sharding import Mesh
from jax.sharding import PartitionSpec as P

HEAD_SIZE = 128
SPAN = 2048
CHUNK = 128
TILE = 256
TILES = SPAN // TILE
GROUP = (4, 2, 1)
BACK_GROUP = (2, 1)
HEADS = 4
ROWS = HEADS * CHUNK
BLOCK_AXES = ("z_lo", "x", "core")
TOKEN_AXES = ("z_lo", "x", "core", "y", "z_hi")
SCALE = 1.0 / math.sqrt(HEAD_SIZE)
LOG2_SCALE = SCALE * math.log2(math.e)
F32, BF16 = jnp.float32, jnp.bfloat16


def dot(a, b, contract):
    return lax.dot_general(a, b, (contract, ((), ())), preferred_element_type=F32)


def rows_of(ref, chunk, part):
    block = ref[chunk, part * CHUNK : (part + 1) * CHUNK]
    return jnp.concatenate(
        [block[:, h * HEAD_SIZE : (h + 1) * HEAD_SIZE] for h in range(HEADS)], axis=0
    )


def store_rows(ref, chunk, value):
    for h in range(HEADS):
        ref[chunk, :, h * HEAD_SIZE : (h + 1) * HEAD_SIZE] = value[h * CHUNK : (h + 1) * CHUNK]


def at(tile, count=1):
    return pl.ds(pl.multiple_of(tile * TILE, TILE), count * TILE)


def sweep(low, high, step, sizes):
    for size in sizes:
        groups = (high - low) // size

        def many(i, _, low=low, size=size):
            step(low + i * size, size)
            return 0

        lax.fori_loop(0, groups, many, 0)
        low = low + groups * size


def own_range(scalars, chunk):
    start = (4 * chunk + scalars[8]) * CHUNK
    low = jnp.maximum(scalars[chunk], 0) // TILE
    high = (start + CHUNK - 1) // TILE + 1
    full_low = jnp.minimum((jnp.maximum(scalars[4 + chunk], 0) + TILE - 1) // TILE, high)
    full_high = jnp.clip((start + 1) // TILE, full_low, high)
    return start, low, high, full_low, full_high


def before_range(scalars, chunk):
    low = jnp.minimum(scalars[chunk] + SPAN, SPAN) // TILE
    full_low = jnp.minimum((scalars[4 + chunk] + SPAN + TILE - 1) // TILE, TILES)
    return low, full_low


def position_in_rows(start):
    return start + (lax.broadcasted_iota(jnp.int32, (1, ROWS), 1) & (CHUNK - 1))


def load_quads(scalars, first, quads, keep):
    span = TILES // 4
    for place, ref in enumerate(quads):
        shift = (scalars[9] ^ place) * span

        def body(tile, _, ref=ref, shift=shift):
            both = ref[at(tile - shift)]
            keep(tile, both[:, :HEAD_SIZE], both[:, HEAD_SIZE:])
            return 0

        lax.fori_loop(jnp.maximum(first, shift), shift + span, body, 0)


def scores(keys, rows_q, tile, count, limits):
    s = LOG2_SCALE * dot(keys, rows_q, ((1,), (1,)))
    if limits is not None:
        begin, last = limits
        key_pos = tile * TILE + lax.broadcasted_iota(jnp.int32, (count * TILE, ROWS), 0)
        allowed = key_pos >= begin
        if last is not None:
            allowed &= key_pos <= last
        s = jnp.where(allowed, s, -1e30)
    return s


def fold(value, how):
    return how(value.reshape(value.shape[0] // 8, 8, ROWS), axis=0)


def own_forward(
    scalars, begin_ref, qd_ref, quad_0, quad_1, quad_2, quad_3,
    stats_ref, out_ref, keys, values_t, probs, top, total,
):
    first = jnp.maximum(scalars[0], 0) // TILE

    def keep(tile, k, v):
        keys[at(tile)] = k
        values_t[:, at(tile)] = v.T

    load_quads(scalars, first, (quad_0, quad_1, quad_2, quad_3), keep)

    def chunk_step(chunk, _):
        start, low, high, full_low, full_high = own_range(scalars, chunk)
        rows_q = rows_of(qd_ref, chunk, 0)
        limits = (begin_ref[chunk], position_in_rows(start))
        top[...] = jnp.full((8, ROWS), -1e30, F32)
        total[...] = jnp.zeros((8, ROWS), F32)
        out_ref[chunk] = jnp.zeros((HEAD_SIZE, ROWS), F32)

        def scores_step(limits):
            def step(tile, count):
                here = at(tile, count)
                s = scores(keys[here], rows_q, tile, count, limits)
                probs[here] = s
                top[...] = jnp.maximum(top[...], fold(s, jnp.max))

            return step

        sweep(low, full_low, scores_step(limits), GROUP)
        sweep(full_low, full_high, scores_step(None), GROUP)
        sweep(full_high, high, scores_step(limits), GROUP)
        row_top = jnp.max(top[...], axis=0, keepdims=True)

        def output_step(tile, count):
            here = at(tile, count)
            p = jnp.exp2(probs[here] - row_top)
            total[...] += fold(p, jnp.sum)
            out_ref[chunk] += dot(values_t[:, here], p.astype(BF16), ((1,), (0,)))

        sweep(low, high, output_step, GROUP)
        stats_ref[chunk, 0:1] = row_top
        stats_ref[chunk, 1:2] = jnp.sum(total[...], axis=0, keepdims=True)
        return 0

    lax.fori_loop(0, 4, chunk_step, 0)


def before_part(
    scalars, begin_ref, qd_ref, quad_0, quad_1, quad_2, quad_3, stats_in, out_in,
    context_ref, grad_ref, handed_ref, keys, values,
    keys_t, values_t, probs, grad_keys, grad_values, out_t, handed, top, total, sem,
):
    first = jnp.minimum(scalars[0] + SPAN, SPAN) // TILE

    def keep(tile, k, v):
        keys[at(tile)] = k
        values[at(tile)] = v
        keys_t[:, at(tile)] = k.T
        values_t[:, at(tile)] = v.T
        grad_keys[at(tile)] = jnp.zeros((TILE, HEAD_SIZE), F32)
        grad_values[at(tile)] = jnp.zeros((TILE, HEAD_SIZE), F32)

    load_quads(scalars, first, (quad_0, quad_1, quad_2, quad_3), keep)

    def blank(tile, _):
        grad_ref[at(tile)] = jnp.zeros((TILE, 2 * HEAD_SIZE), BF16)
        return 0

    lax.fori_loop(0, first, blank, 0)

    def hand_over(chunk):
        return pltpu.make_async_copy(
            handed.at[chunk], handed_ref.at[chunk], sem.at[chunk]
        )

    def chunk_step(chunk, _):
        low, full_low = before_range(scalars, chunk)
        rows_q = rows_of(qd_ref, chunk, 0)
        rows_d = rows_of(qd_ref, chunk, 1)
        limits = (begin_ref[chunk] + SPAN, None)
        own_top, own_total = stats_in[chunk, 0:1], stats_in[chunk, 1:2]
        top[...] = jnp.broadcast_to(own_top, (8, ROWS))
        total[...] = jnp.zeros((8, ROWS), F32)
        handed[chunk, :HEAD_SIZE] = jnp.zeros((HEAD_SIZE, ROWS), F32)

        def scores_step(limits):
            def step(tile, count):
                here = at(tile, count)
                s = scores(keys[here], rows_q, tile, count, limits)
                probs[here] = s
                top[...] = jnp.maximum(top[...], fold(s, jnp.max))

            return step

        sweep(low, full_low, scores_step(limits), GROUP)
        sweep(full_low, TILES, scores_step(None), GROUP)
        row_top = jnp.max(top[...], axis=0, keepdims=True)
        rescale = jnp.exp2(own_top - row_top)
        out_t[...] = out_in[chunk] * rescale

        def output_step(tile, count):
            here = at(tile, count)
            p = jnp.exp2(probs[here] - row_top)
            probs[here] = p
            total[...] += fold(p, jnp.sum)
            out_t[...] += dot(values_t[:, here], p.astype(BF16), ((1,), (0,)))

        sweep(low, TILES, output_step, GROUP)
        row_total = jnp.sum(total[...], axis=0, keepdims=True) + own_total * rescale
        inverse = 1.0 / row_total
        attended = out_t[...] * inverse
        delta = jnp.sum(rows_d.T.astype(F32) * attended, axis=0, keepdims=True)
        store_rows(context_ref, (chunk - scalars[9]) & 3, attended.astype(BF16).T)
        handed[chunk, HEAD_SIZE : HEAD_SIZE + 1] = row_top + jnp.log2(row_total)
        handed[chunk, HEAD_SIZE + 1 : HEAD_SIZE + 2] = delta

        def gradient_step(tile, count):
            here = at(tile, count)
            w = probs[here] * inverse
            grad_weights = dot(values[here], rows_d, ((1,), (1,)))
            grad_scores = (w * (grad_weights - delta)).astype(BF16)
            grad_values[here] += dot(w.astype(BF16), rows_d, ((1,), (0,)))
            grad_keys[here] += dot(grad_scores, rows_q, ((1,), (0,)))
            handed[chunk, :HEAD_SIZE] += dot(keys_t[:, here], grad_scores, ((1,), (0,)))

        sweep(low, TILES, gradient_step, GROUP)
        hand_over(chunk).start()
        return 0

    lax.fori_loop(0, 4, chunk_step, 0)

    def store(tile, _):
        grad_ref[at(tile), :HEAD_SIZE] = (grad_keys[at(tile)] * SCALE).astype(BF16)
        grad_ref[at(tile), HEAD_SIZE:] = grad_values[at(tile)].astype(BF16)
        return 0

    lax.fori_loop(first, TILES, store, 0)
    for chunk in range(4):
        hand_over(chunk).wait()


def own_backward(
    scalars, begin_ref, qd_ref, quad_0, quad_1, quad_2, quad_3, handed_in, context_in,
    out_0, out_1, out_2, out_3, grad_ref, keys, values,
    keys_t, grad_keys, grad_values, handed, grad_query, sem,
):
    first = jnp.maximum(scalars[0], 0) // TILE

    def fetch(chunk):
        return pltpu.make_async_copy(
            handed_in.at[chunk], handed.at[chunk], sem.at[chunk]
        )

    for chunk in range(4):
        fetch(chunk).start()

    def keep(tile, k, v):
        keys[at(tile)] = k
        values[at(tile)] = v
        keys_t[:, at(tile)] = k.T
        grad_keys[at(tile)] = jnp.zeros((TILE, HEAD_SIZE), F32)
        grad_values[at(tile)] = jnp.zeros((TILE, HEAD_SIZE), F32)

    load_quads(scalars, first, (quad_0, quad_1, quad_2, quad_3), keep)

    def blank(tile, _):
        grad_ref[at(tile)] = jnp.zeros((TILE, 2 * HEAD_SIZE), BF16)
        return 0

    lax.fori_loop(0, first, blank, 0)

    def chunk_step(chunk, _):
        start, low, high, full_low, full_high = own_range(scalars, chunk)
        rows_q = rows_of(qd_ref, chunk, 0)
        rows_d = rows_of(qd_ref, chunk, 1)
        limits = (begin_ref[chunk], position_in_rows(start))
        fetch(chunk).wait()
        log_total = handed[chunk, HEAD_SIZE : HEAD_SIZE + 1]
        delta = handed[chunk, HEAD_SIZE + 1 : HEAD_SIZE + 2]

        def gradient_step(limits):
            def step(tile, count):
                here = at(tile, count)
                s = scores(keys[here], rows_q, tile, count, limits)
                w = jnp.exp2(s - log_total)
                grad_weights = dot(values[here], rows_d, ((1,), (1,)))
                grad_scores = (w * (grad_weights - delta)).astype(BF16)
                grad_values[here] += dot(w.astype(BF16), rows_d, ((1,), (0,)))
                grad_keys[here] += dot(grad_scores, rows_q, ((1,), (0,)))
                handed[chunk, :HEAD_SIZE] += dot(keys_t[:, here], grad_scores, ((1,), (0,)))

            return step

        sweep(low, full_low, gradient_step(limits), BACK_GROUP)
        sweep(full_low, full_high, gradient_step(None), BACK_GROUP)
        sweep(full_high, high, gradient_step(limits), BACK_GROUP)
        store_rows(grad_query, (chunk - scalars[9]) & 3, (handed[chunk, :HEAD_SIZE] * SCALE).astype(BF16).T)
        return 0

    lax.fori_loop(0, 4, chunk_step, 0)

    def store(tile, _):
        grad_ref[at(tile), :HEAD_SIZE] = (grad_keys[at(tile)] * SCALE).astype(BF16)
        grad_ref[at(tile), HEAD_SIZE:] = grad_values[at(tile)].astype(BF16)
        return 0

    lax.fori_loop(first, TILES, store, 0)
    for slot, out in enumerate((out_0, out_1, out_2, out_3)):
        out[:CHUNK] = context_in[slot]
        out[CHUNK:] = grad_query[slot]


def call(kernel, name, gflops, megabytes, outs, scratch, *args, hbm_in=(), hbm_out=(), sems=0):
    vmem, hbm = pl.BlockSpec(memory_space=pltpu.VMEM), pl.BlockSpec(memory_space=pltpu.HBM)
    return pl.pallas_call(
        kernel,
        out_shape=tuple(jax.ShapeDtypeStruct(shape, dtype) for shape, dtype in outs),
        in_specs=[pl.BlockSpec(memory_space=pltpu.SMEM)]
        + [hbm if n in hbm_in else vmem for n in range(1, len(args))],
        out_specs=tuple(hbm if n in hbm_out else vmem for n in range(len(outs))),
        scratch_shapes=[pltpu.VMEM(shape, dtype) for shape, dtype in scratch]
        + ([pltpu.SemaphoreType.DMA((sems,))] if sems else []),
        compiler_params=pltpu.CompilerParams(vmem_limit_bytes=megabytes << 20),
        cost_estimate=pl.CostEstimate(
            flops=gflops * 10**9, bytes_accessed=4 << 20, transcendentals=2 * 10**6
        ),
        name=name,
    )(*args)


STATS = ((4, 2, ROWS), F32)
ACROSS = ((4, HEAD_SIZE, ROWS), F32)
HANDED = ((4, HEAD_SIZE + 8, ROWS), F32)
RESULT = ((4, CHUNK, ROWS), BF16)
PIECE = ((2 * CHUNK, ROWS), BF16)
GRADS = ((SPAN, 2 * HEAD_SIZE), BF16)
LINES = ((SPAN, HEAD_SIZE), BF16)
TURNED = ((HEAD_SIZE, SPAN), BF16)
SQUARE = ((SPAN, ROWS), F32)
SUMS = ((SPAN, HEAD_SIZE), F32)
FLAT = ((HEAD_SIZE, ROWS), F32)
EIGHT = ((8, ROWS), F32)


def run_own_forward(scalars, begin, qd, kv):
    return call(
        own_forward, "own_forward", 2, 12, (STATS, ACROSS), (LINES, TURNED, SQUARE, EIGHT, EIGHT),
        scalars, begin, qd, *kv,
    )


def run_before_part(scalars, begin, qd, kv, stats, out):
    return call(
        before_part, "before_part", 2, 18, (RESULT, GRADS, HANDED),
        (LINES, LINES, TURNED, TURNED, SQUARE, SUMS, SUMS, FLAT, HANDED, EIGHT, EIGHT),
        scalars, begin, qd, *kv, stats, out, hbm_out=(2,), sems=4,
    )


def run_own_backward(scalars, begin, qd, kv, handed, context):
    return call(
        own_backward, "own_backward", 3, 60, (PIECE,) * 4 + (GRADS,),
        (LINES, LINES, TURNED, SUMS, SUMS, HANDED, RESULT),
        scalars, begin, qd, *kv, handed, context, hbm_in=(7,), sems=4,
    )


def small(kernel, name, outs, scalar, *args):
    vmem = pl.BlockSpec(memory_space=pltpu.VMEM)
    smem = [pl.BlockSpec(memory_space=pltpu.SMEM)] if scalar is not None else []
    return pl.pallas_call(
        kernel,
        out_shape=tuple(jax.ShapeDtypeStruct(shape, dtype) for shape, dtype in outs),
        in_specs=smem + [vmem] * len(args),
        out_specs=tuple(vmem for _ in outs),
        compiler_params=pltpu.CompilerParams(vmem_limit_bytes=8 << 20),
        cost_estimate=pl.CostEstimate(flops=10**6, bytes_accessed=2 << 20, transcendentals=0),
        name=name,
    )(*([scalar] if scalar is not None else []), *args)


def copy_all(moves, sem):
    copies = [
        pltpu.make_async_copy(source, target, sem.at[n]) for n, (source, target) in enumerate(moves)
    ]
    for copy in copies:
        copy.start()
    for copy in copies:
        copy.wait()


def packing(kernel, name, outs, scalar, *args, sems):
    hbm, vmem = pl.BlockSpec(memory_space=pltpu.HBM), pl.BlockSpec(memory_space=pltpu.VMEM)
    smem = [pl.BlockSpec(memory_space=pltpu.SMEM)] if scalar is not None else []
    return pl.pallas_call(
        kernel,
        out_shape=tuple(jax.ShapeDtypeStruct(shape, dtype) for shape, dtype in outs),
        in_specs=smem + [hbm] * len(args),
        out_specs=(vmem,) * len(outs),
        scratch_shapes=[pltpu.SemaphoreType.DMA((sems,))],
        compiler_params=pltpu.CompilerParams(vmem_limit_bytes=60 << 20),
        cost_estimate=pl.CostEstimate(flops=10**6, bytes_accessed=2 << 20, transcendentals=0),
        name=name,
    )(*([scalar] if scalar is not None else []), *args)


def pack_rows(queries, output_gradient):
    def kernel(q_ref, d_ref, qd_ref, sem):
        copy_all(
            [
                (
                    source.at[:, pl.ds(d * ROWS, ROWS)],
                    qd_ref.at[d, pl.ds(index * CHUNK, CHUNK)],
                )
                for index, source in enumerate((q_ref, d_ref))
                for d in range(4)
            ],
            sem,
        )

    outs = (((4, 2 * CHUNK, ROWS), BF16),)
    return packing(kernel, "pack_rows", outs, None, queries, output_gradient, sems=8)[0]


def pack_heads(y, keys, values):
    def kernel(y_ref, k_ref, v_ref, out_ref, sem):
        mine = y_ref[0] >> 1
        copy_all(
            [
                (
                    source.at[:, pl.ds(pl.multiple_of(head * HEAD_SIZE, HEAD_SIZE), HEAD_SIZE)],
                    out_ref.at[slot, :, pl.ds(index * HEAD_SIZE, HEAD_SIZE)],
                )
                for index, source in enumerate((k_ref, v_ref))
                for slot, head in enumerate((mine, 1 - mine))
            ],
            sem,
        )

    outs = (((2, CHUNK, 2 * HEAD_SIZE), BF16),)
    return packing(kernel, "pack_heads", outs, y, keys, values, sems=4)[0]


def pair_sum(grad):
    def kernel(grad_ref, out_ref):
        for place in range(4):
            for head in range(2):
                out_ref[place, head] = (
                    grad_ref[2 * head, place].astype(F32) + grad_ref[2 * head + 1, place].astype(F32)
                ).astype(BF16)

    return small(kernel, "pair_sum", (((4, 2, CHUNK, 2 * HEAD_SIZE), BF16),), None, grad)[0]


def join(y, *pieces):
    def kernel(y_ref, *refs):
        context_ref, grad_ref = refs[4:]
        for step in range(4):
            group = (y_ref[0] - step) & 3
            here = pl.ds(pl.multiple_of(group * ROWS, ROWS), ROWS)
            context_ref[:, here] = refs[step][:CHUNK]
            grad_ref[:, here] = refs[step][CHUNK:]

    return small(kernel, "join", (((CHUNK, 4 * ROWS), BF16),) * 2, y, *pieces)


def last_sum(grad):
    def kernel(grad_ref, keys_ref, values_ref):
        for head in range(2):
            total = sum(grad_ref[i, head].astype(F32) for i in range(4)).astype(BF16)
            here = slice(head * HEAD_SIZE, (head + 1) * HEAD_SIZE)
            keys_ref[:, here] = total[:, :HEAD_SIZE]
            values_ref[:, here] = total[:, HEAD_SIZE:]

    outs = (((CHUNK, 2 * HEAD_SIZE), BF16),) * 2
    return small(kernel, "last_sum", outs, None, grad)


def columns(value, index, count):
    width = value.shape[1] // count
    return value[:, index * width : (index + 1) * width]


def per_device(queries, key_projection, value_projection, output_gradient, doc_lengths):
    z_hi = lax.axis_index("z_hi").astype(jnp.int32)
    y = lax.axis_index("y").astype(jnp.int32)
    block = lax.axis_index(BLOCK_AXES).astype(jnp.int32)
    blocks = lax.axis_size(BLOCK_AXES)
    own_start = block * SPAN
    kv = pack_heads(y[None], key_projection, value_projection)
    qd = pack_rows(queries, output_gradient)
    qd = lax.all_to_all(qd, "y", split_axis=0, concat_axis=0, tiled=True)
    kv = lax.all_gather(kv, "z_hi", axis=1, tiled=True)
    qd, kv = lax.optimization_barrier((qd, kv))
    across = [(i, i ^ 3) for i in range(4)]
    beside = [(i, i ^ 1) for i in range(4)]
    to_next = [(i, i + 1) for i in range(blocks - 1)]
    quad_0 = kv[0]
    quad_3 = lax.ppermute(kv[1], "y", across)
    quad_1 = lax.ppermute(quad_0, "y", beside)
    quad_2 = lax.ppermute(quad_3, "y", beside)
    kv_own = (quad_0, quad_1, quad_2, quad_3)
    kv_before = tuple(lax.ppermute(quad, BLOCK_AXES, to_next) for quad in kv_own)
    docs = doc_lengths.shape[0]
    order = jnp.arange(docs)
    starts = jnp.sum(jnp.where(order[None, :] < order[:, None], doc_lengths[None, :], 0), axis=1)
    chunk_start = (4 * jnp.arange(4, dtype=jnp.int32) + z_hi) * CHUNK + own_start
    position = (chunk_start[:, None] + jnp.arange(CHUNK, dtype=jnp.int32)[None, :])[..., None]
    begin = jnp.max(jnp.where(starts <= position, starts, 0), axis=2).astype(jnp.int32) - own_start
    scalars = jnp.concatenate([begin[:, 0], begin[:, -1], z_hi[None], y[None]])
    begin = jnp.tile(begin, (1, HEADS)).reshape(4, 1, ROWS)

    stats, out = run_own_forward(scalars, begin, qd, kv_own)
    kv_before, stats, out = lax.optimization_barrier((kv_before, stats, out))
    context, grad_before, handed = run_before_part(
        scalars, begin, qd, kv_before, stats, out
    )
    returned = lax.ppermute(grad_before, BLOCK_AXES, [(i + 1, i) for i in range(blocks - 1)])
    *results, grad_own = run_own_backward(scalars, begin, qd, kv_own, handed, context)
    grad_own = (grad_own.astype(F32) + returned.astype(F32)).astype(BF16)
    grad = lax.all_to_all(
        grad_own.reshape(4, 4, CHUNK, 2 * HEAD_SIZE), "y", split_axis=0, concat_axis=0, tiled=True
    )

    grad = pair_sum(grad)
    grad, *results = lax.optimization_barrier((grad, *results))
    grad = lax.all_to_all(grad, "z_hi", split_axis=0, concat_axis=0, tiled=True)
    pieces = [results[0]] + [
        lax.ppermute(results[step], "y", [(i, (i + step) % 4) for i in range(4)])
        for step in (1, 2, 3)
    ]
    context, grad_queries = join(y[None], *pieces)
    keys_gradient, values_gradient = last_sum(grad)
    return (
        context,
        grad_queries,
        keys_gradient,
        values_gradient,
    )


def solution(mesh):
    order = [mesh.axis_names.index(name) for name in ("uly", "blk")]
    devices = np.transpose(mesh.devices, order).reshape(4, 4, 4, 4, 2)
    fine = Mesh(devices, ("y", "z_hi", "z_lo", "x", "core"))
    rows = P(TOKEN_AXES, None)
    return jax.shard_map(
        per_device, mesh=fine, in_specs=(rows, rows, rows, rows, P()),
        out_specs=(rows, rows, rows, rows), check_vma=False,
    )
```
